128 devices in a mesh: shot: 8 (over x, z_hi), dom: 16 (over z_lo, y, core).
Axes of the slice: x: 4, y: 4, z: 4 (z_hi: 2, z_lo: 2; z = z_hi * 2 + z_lo), core: 2. Of those that a mesh axis runs over, the one named last changes fastest.
Arguments:
- velocity: float32 [512, 32, 128], P('dom'), may hold values from 1.5 to 3
- noise_field: float32 [512, 32, 128], P('dom'), may hold values from -6 to 6
- step_size: float32 [1], replicated, may hold values from 0.05 to 0.5
- field_prev: float32 [16, 512, 32, 128], P('shot', 'dom'), may hold values from -6 to 6
- field_now: float32 [16, 512, 32, 128], P('shot', 'dom'), may hold values from -6 to 6
- adjoint_next: float32 [16, 512, 32, 128], P('shot', 'dom'), may hold values from -6 to 6
- adjoint_now: float32 [16, 512, 32, 128], P('shot', 'dom'), may hold values from -6 to 6
- wavelet: float32 [16, 4], P('shot'), may hold values from -8 to 8
- source_cells: int32 [16, 8], P('shot'), may hold values from 0 to 2097151
- source_signs: int32 [16, 8], P('shot'), may hold values from 0 to 1
- record_cells: int32 [16, 256], P('shot'), may hold values from 0 to 2097151
- observed: float32 [16, 4, 256], P('shot'), may hold values from -6 to 6
Outputs:
- new_velocity: float32 [512, 32, 128], P('dom', None, 'shot')
The draws below stay inside these ranges and needn't reach their ends.
Inputs may be any that keep to these rules, and one draw needn't show every extreme that they name: `source_signs`: 0 stands for a negative sign, 1 for a positive one. `source_cells`: cells flattened as x 32 * 128 + z * 128 + y. `record_cells`: cells flattened as x 32 * 128 + z * 128 + y.
All inputs are finite; a program needn't handle non-finite values.
Results may differ from the reference program's by a relative error of at most 0.00009.
Values sent between devices are 32-bit elements; how exact they have to be, the bound alone decides.
No kernel may reach another device: no remote copies, remote signals or barrier semaphores. Data moves between devices by JAX's collectives and lax.ppermute only.
A program may use at most 128 MiB of HBM per device.

```python
import math
import jax
import jax.numpy as jnp
from jax import lax

NZ = 32
NY = 128
STEPS = 4
NSRC = 8
NREC = 256
NX = 512
SHOTS = 16
KC = 16


def draw_noise_field(key, part):
    sample = jax.random.normal(key, (NX, NZ, NY), jnp.float32)
    return jnp.clip(sample, -5.0, 5.0)


def touch_ends(result, rng, least, largest):
    longest = result.shape.index(max(result.shape))
    spots = []
    for shift in (0, 1):
        where = [jax.random.randint(jax.random.fold_in(rng, axis), (), 0, length) for axis, length in enumerate(result.shape)]
        where[longest] = (where[longest] + shift) % result.shape[longest]
        spots.append(tuple(where))
    return result.at[spots[0]].set(least).at[spots[1]].set(largest)


def shard_levels(key, dims, pieces, smallest, top_value):
    factor_of, own = 1.0, jax.random.fold_in(key, 6)
    for dim, shards_of in pieces:
        draws = jnp.exp(jax.random.uniform(jax.random.fold_in(own, dim), (shards_of,), jnp.float32, smallest / len(pieces), top_value / len(pieces)))
        factor_of = factor_of * jnp.repeat(draws, dims[dim] // shards_of).reshape([-1 if axis == dim else 1 for axis in range(len(dims))])
    return factor_of


def centred(stream_key, extent, width, reach, cuts=(), kind=jnp.bfloat16):
    values = width * jax.random.normal(stream_key, extent, jnp.float32)
    if cuts:
        values = values * shard_levels(stream_key, extent, cuts, -0.22, 0.18)
    return jnp.clip(values, -reach, reach).astype(kind)


def setup_inputs(seed: int = 0) -> dict:
    key_of = jax.random.split(jax.random.key(seed), 13)
    return {
        "velocity": jnp.clip(1.5 + 1.5 * jax.random.uniform(key_of[0], (NX, NZ, NY), jnp.float32) ** shard_levels(key_of[0], (NX, NZ, NY), ((0, 16),), -0.2, 0.2), 1.5, 3.0),
        "noise_field": draw_noise_field(jax.random.fold_in(key_of[12], 71), 0),
        "step_size": jnp.clip(jnp.exp(jax.random.uniform(key_of[2], (1,), jnp.float32, math.log(0.05), math.log(0.5))), 0.05, 0.5),
        "field_prev": centred(key_of[3], (SHOTS, NX, NZ, NY), 1.0, 6.0, ((0, 8), (1, 16)), jnp.float32),
        "field_now": centred(key_of[4], (SHOTS, NX, NZ, NY), 1.0, 6.0, ((0, 8), (1, 16)), jnp.float32),
        "adjoint_next": centred(key_of[5], (SHOTS, NX, NZ, NY), 1.0, 6.0, ((0, 8), (1, 16)), jnp.float32),
        "adjoint_now": centred(key_of[6], (SHOTS, NX, NZ, NY), 1.0, 6.0, ((0, 8), (1, 16)), jnp.float32),
        "wavelet": centred(key_of[7], (SHOTS, STEPS), 2.0, 8.0, ((0, 8),), jnp.float32),
        "source_cells": touch_ends(jax.random.randint(key_of[8], (SHOTS, NSRC), 0, NX * NY * NZ), jax.random.fold_in(key_of[8], 1), 0, (NX * NY * NZ) - 1).astype(jnp.int32),
        "source_signs": touch_ends(jax.random.randint(key_of[9], (SHOTS, NSRC), 0, 2), jax.random.fold_in(key_of[9], 1), 0, 1).astype(jnp.int32),
        "record_cells": touch_ends(jax.random.randint(key_of[10], (SHOTS, NREC), 0, NX * NY * NZ), jax.random.fold_in(key_of[10], 1), 0, (NX * NY * NZ) - 1).astype(jnp.int32),
        "observed": centred(key_of[11], (SHOTS, STEPS, NREC), 1.0, 6.0, ((0, 8),), jnp.float32),
    }


COEFFS = (-205.0 / 72.0, 8.0 / 5.0, -1.0 / 5.0, 8.0 / 315.0, -1.0 / 560.0)
COURANT = 0.02

def stencil(padded):
    margin = 4
    rank = padded.ndim
    lengths = [padded.shape[rank - 3 + place] - 2 * margin for place in range(3)]

    def window(offsets):
        sliced = padded
        for place in range(3):
            begin = margin + offsets[place]
            sliced = lax.slice_in_dim(sliced, begin, begin + lengths[place], axis=rank - 3 + place)
        return sliced
    summed = 3.0 * COEFFS[0] * window((0, 0, 0))
    for distance in range(1, 5):
        beside_all = window((distance, 0, 0)) + window((-distance, 0, 0))
        beside_all = beside_all + window((0, distance, 0)) + window((0, -distance, 0))
        beside_all = beside_all + window((0, 0, distance)) + window((0, 0, -distance))
        summed = summed + COEFFS[distance] * beside_all
    return summed

def cosine_basis(length):
    wave_index = jnp.arange(length, dtype=jnp.int32)[:, None]
    position = jnp.arange(length, dtype=jnp.int32)[None, :]
    phase = wave_index * (2 * position + 1) % (4 * length)
    angle = math.pi / (2.0 * length) * phase.astype(jnp.float32)
    factor = jnp.where(wave_index == 0, math.sqrt(1.0 / length), math.sqrt(2.0 / length)).astype(jnp.float32)
    return factor * jnp.cos(angle)

def prior_gain(length, cutoff):
    scaled = jnp.arange(length, dtype=jnp.float32) / float(cutoff)
    return 1.0 / jnp.sqrt(1.0 + scaled)

def reference(velocity, noise_field, step_size, field_prev, field_now, adjoint_next, adjoint_now, wavelet, source_cells, source_signs, record_cells, observed):
    speed_sq = COURANT * velocity * velocity
    grid_shape = velocity.shape

    def one_shot(carry, inputs):
        prior, current, adj_later, adj_current, pulse, sources, signs, records, measured = inputs
        amplitude = (2 * signs - 1).astype(jnp.float32)
        laplacians = []
        samples = []
        for moment in range(STEPS):
            spread = stencil(jnp.pad(current, 4))
            laplacians.append(spread)
            advanced = 2.0 * current - prior + speed_sq * spread
            advanced = advanced.reshape(-1).at[sources].add(amplitude * pulse[moment]).reshape(grid_shape)
            samples.append(advanced.reshape(-1)[records])
            prior, current = (current, advanced)
        summed = jnp.zeros(grid_shape, jnp.float32)
        for moment in range(STEPS, 0, -1):
            misfit = samples[moment - 1] - measured[moment - 1]
            spread = stencil(jnp.pad(adj_current, 4))
            earlier = 2.0 * adj_current - adj_later + speed_sq * spread
            earlier = earlier.reshape(-1).at[records].add(misfit).reshape(grid_shape)
            adj_later, adj_current = (adj_current, earlier)
            summed = summed + adj_current * laplacians[moment - 1]
        return (carry + summed, None)
    start_total = jnp.zeros(grid_shape, jnp.float32)
    total = lax.scan(one_shot, start_total, (field_prev, field_now, adjoint_next, adjoint_now, wavelet, source_cells, source_signs, record_cells, observed))[0]
    gradient = 2.0 * COURANT * velocity * total
    basis = cosine_basis(NX)
    spectrum = prior_gain(NX, KC)[:, None]
    columns = NY * NZ
    highest = lax.Precision.HIGHEST
    grad_hat = jnp.dot(basis, gradient.reshape(NX, columns), precision=highest)
    noise_hat = jnp.dot(basis, noise_field.reshape(NX, columns), precision=highest)
    rate = step_size[0]
    weights = spectrum * (-0.5 * rate * spectrum * grad_hat + jnp.sqrt(rate) * noise_hat)
    update = lax.dot_general(basis, weights, (((0,), (0,)), ((), ())), precision=highest)
    return velocity + update.reshape(NX, NZ, NY)
```

```python
import math

import jax
import jax.numpy as jnp
import ml_dtypes
import numpy as np
from jax import lax
from jax.experimental import pallas as pl
from jax.experimental.pallas import tpu as pltpu
from jax.sharding import PartitionSpec as P

STEPS = 4
COEFFS = (-205.0 / 72.0, 8.0 / 5.0, -1.0 / 5.0, 8.0 / 315.0, -1.0 / 560.0)
COURANT = 0.02
CUTOFF = 16

NX, NZ, NY = 512, 32, 128
SLAB = 32
DEEP = 16
SHALLOW = 12
ROWS = SLAB + 2 * DEEP
PAD = 8
DEPTH = NZ + 2 * PAD
SHOTS_HERE = 2
NREC = 256
LIST = NREC + 8
CHUNK = 8
VMEM_LIMIT = 56 * 1024 * 1024

ANY = pl.BlockSpec(memory_space=pl.ANY)
VMEM = pl.BlockSpec(memory_space=pltpu.VMEM)
SMEM = pl.BlockSpec(memory_space=pltpu.SMEM)


def split_host(matrix):
    high = matrix.astype(ml_dtypes.bfloat16)
    low = (matrix - high.astype(np.float64)).astype(ml_dtypes.bfloat16)
    return high, low


def lane_operator():
    band = np.zeros((NY, NY))
    np.fill_diagonal(band, 3.0 * COEFFS[0])
    for distance in range(1, 5):
        band += COEFFS[distance] * (np.eye(NY, k=distance) + np.eye(NY, k=-distance))
    high, low = split_host(band)
    zero = np.zeros_like(low)
    return np.block([[high, low], [high, zero]])


def prior_operators():
    wave = np.arange(NX)[:, None]
    position = np.arange(NX)[None, :]
    factor = np.where(wave == 0, math.sqrt(1.0 / NX), math.sqrt(2.0 / NX))
    basis = factor * np.cos(math.pi / (2.0 * NX) * (wave * (2 * position + 1) % (4 * NX)))
    gain = 1.0 / np.sqrt(1.0 + np.arange(NX) / CUTOFF)
    squared = basis.T @ (gain[:, None] ** 2 * basis)
    single = basis.T @ (gain[:, None] * basis)
    return np.stack([*split_host(squared), *split_host(single)])


def split(values):
    high = values.astype(jnp.bfloat16)
    low = (values - high.astype(jnp.float32)).astype(jnp.bfloat16)
    return high, low


def dot(left, right):
    return jnp.dot(left, right, preferred_element_type=jnp.float32)


def prepare_kernel(rec, row_out, lane_out, index_out, count_out):
    base = (lax.axis_index("dom") * SLAB - DEEP) * (NZ * NY)
    first = (DEEP - SHALLOW) * NZ * NY
    last = (DEEP + SLAB + SHALLOW) * NZ * NY
    for shot in range(SHOTS_HERE):

        def gather(item, count, shot=shot):
            cell = rec[shot, item] - base
            inside = (cell >= first) & (cell < last)
            row_out[shot, count] = cell >> 7
            lane_out[shot, count] = cell & 127
            index_out[shot, count] = item
            return count + inside.astype(jnp.int32)

        count = lax.fori_loop(0, NREC, gather, jnp.int32(0), unroll=8)
        for extra in range(4):
            row_out[shot, count + extra] = DEEP * NZ
            lane_out[shot, count + extra] = -1
            index_out[shot, count + extra] = 0
        count_out[shot] = (count + 3) >> 2


def clear_pads(fields, number):
    zeros = jnp.zeros((ROWS, PAD, NY), jnp.float32)
    for field in range(1, number):
        for shot in range(SHOTS_HERE):
            fields[field, shot, :, 0:PAD, :] = zeros
            fields[field, shot, :, PAD + NZ : DEPTH, :] = zeros


def load_field(fields, field, own, low, high, offset, width, sems, base):
    copies = []
    begin = DEEP - width
    for shot in range(SHOTS_HERE):
        planes = pl.ds(offset + shot * width, width)
        view = fields.at[field, shot]
        for number, (source, target) in enumerate(
            (
                (low.at[planes], view.at[pl.ds(begin, width), pl.ds(PAD, NZ), :]),
                (own.at[shot], view.at[pl.ds(DEEP, SLAB), pl.ds(PAD, NZ), :]),
                (high.at[planes], view.at[pl.ds(DEEP + SLAB, width), pl.ds(PAD, NZ), :]),
            )
        ):
            copies.append(pltpu.make_async_copy(source, target, sems.at[base + shot * 3 + number]))
    return copies


def load_speed(speed, own, low, high, offset, sems, base):
    planes = pl.ds(offset, SHALLOW)
    return [
        pltpu.make_async_copy(low.at[planes], speed.at[pl.ds(DEEP - SHALLOW, SHALLOW)], sems.at[base]),
        pltpu.make_async_copy(own, speed.at[pl.ds(DEEP, SLAB)], sems.at[base + 1]),
        pltpu.make_async_copy(high.at[planes], speed.at[pl.ds(DEEP + SLAB, SHALLOW)], sems.at[base + 2]),
    ]


def square_speed(speed):
    @pl.loop(0, (SLAB + 2 * SHALLOW) // 8)
    def _(part):
        rows = pl.ds(DEEP - SHALLOW + part * 8, 8)
        value = speed[rows]
        speed[rows] = COURANT * value * value


def leap(fields, speed, lanes, source, margin, laplacians=None, slot=None):
    first = DEEP - margin
    chunks = (SLAB + 2 * margin) // CHUNK

    @pl.loop(0, SHOTS_HERE * chunks)
    def _(item):
        shot = item // chunks
        begin = first + (item % chunks) * CHUNK
        block = fields[source, shot, pl.ds(begin, CHUNK), PAD : PAD + NZ, :].reshape(CHUNK * NZ, NY)
        along = dot(jnp.concatenate(split(block), axis=1), lanes[...])
        for plane in range(CHUNK):
            here = begin + plane
            part = along[plane * NZ : (plane + 1) * NZ]
            spread = part[:, :NY] + part[:, NY:]
            for distance in range(1, 5):
                beside = (
                    fields[source, shot, here + distance, PAD : PAD + NZ, :]
                    + fields[source, shot, here - distance, PAD : PAD + NZ, :]
                ) + (
                    fields[source, shot, here, PAD + distance : PAD + NZ + distance, :]
                    + fields[source, shot, here, PAD - distance : PAD + NZ - distance, :]
                )
                spread = spread + COEFFS[distance] * beside
            centre = fields[source, shot, here, PAD : PAD + NZ, :]
            before = fields[source - 1, shot, here, PAD : PAD + NZ, :]
            fields[source + 1, shot, here, PAD : PAD + NZ, :] = (
                2.0 * centre - before + speed[here] * spread
            )
            if laplacians is not None:
                laplacians[slot, shot, here] = spread


def lane_ids():
    return lax.broadcasted_iota(jnp.int32, (1, NY), 1)


def forward_kernel(
    rows, lanes_of, index, counts, src, signs, wave,
    now, prev, vel, low, high, lanes,
    lap_out, samples,
    fields, laps, speed, sems, out_sems,
):
    copies = load_field(fields, 1, now, low, high, 0, DEEP, sems, 0)
    copies += load_field(fields, 0, prev, low, high, 2 * DEEP, SHALLOW, sems, 6)
    copies += load_speed(speed, vel, low, high, 2 * DEEP + 2 * SHALLOW, sems, 12)
    for copy in copies:
        copy.start()
    clear_pads(fields, 5)
    for copy in copies:
        copy.wait()
    square_speed(speed)
    base = (lax.axis_index("dom") * SLAB - DEEP) * (NZ * NY)
    ids = lane_ids()
    outs = []
    for moment in range(STEPS):
        margin = 4 * (STEPS - 1 - moment)
        leap(fields, speed, lanes, moment + 1, margin, laps, moment)
        out = pltpu.make_async_copy(laps.at[moment, :, pl.ds(DEEP, SLAB)], lap_out.at[moment], out_sems.at[moment])
        out.start()
        outs.append(out)
        first = (DEEP - margin) * NZ * NY
        last = (DEEP + SLAB + margin) * NZ * NY
        for shot in range(SHOTS_HERE):

            @pl.loop(0, src.shape[1])
            def _(item, shot=shot):
                cell = src[shot, item] - base

                @pl.when((cell >= first) & (cell < last))
                def _():
                    amplitude = (2 * signs[shot, item] - 1).astype(jnp.float32) * wave[shot, moment]
                    plane = cell >> 12
                    depth = PAD + ((cell >> 7) & (NZ - 1))
                    view = fields.at[moment + 2, shot, plane, pl.ds(depth, 1), :]
                    view[...] = view[...] + jnp.where(ids == (cell & 127), amplitude, 0.0)

    for shot in range(SHOTS_HERE):

        def sample(group, state, shot=shot):
            state = list(state)
            for member in range(4):
                item = group * 4 + member
                row, lane, which = rows[shot, item], lanes_of[shot, item], index[shot, item]
                plane = row >> 5
                depth = PAD + (row & (NZ - 1))
                own = (lane >= 0) & (plane >= DEEP) & (plane < DEEP + SLAB)
                shift = (which - lane) & 127
                for half in range(2):
                    hit = ids == jnp.where(own, which - half * NY, -1)
                    for moment in range(STEPS):
                        line = fields[moment + 2, shot, plane, pl.ds(depth, 1), :]
                        line = pltpu.roll(line, shift, 1)
                        state[moment * 2 + half] = jnp.where(hit, line, state[moment * 2 + half])
            return tuple(state)

        zero = jnp.zeros((1, NY), jnp.float32)
        state = lax.fori_loop(0, counts[shot], sample, (zero,) * (2 * STEPS))
        for moment in range(STEPS):
            for half in range(2):
                line = shot * STEPS + moment
                samples[line : line + 1, half * NY : (half + 1) * NY] = state[moment * 2 + half]
    for out in outs:
        out.wait()


def adjoint_kernel(
    rows, lanes_of, index, counts, misfit,
    now, after, vel, low, high, vel_low, vel_high, laps_in, lanes,
    tiles,
    fields, laps, speed, plain, grad, sems,
):
    copies = load_field(fields, 1, now, low, high, 0, DEEP, sems, 0)
    copies += load_field(fields, 0, after, low, high, 2 * DEEP, SHALLOW, sems, 6)
    copies += load_speed(speed, vel, vel_low, vel_high, 2 * DEEP + 2 * SHALLOW, sems, 12)
    late = [
        pltpu.make_async_copy(laps_in, laps, sems.at[15]),
        pltpu.make_async_copy(vel, plain, sems.at[16]),
    ]
    for copy in copies + late:
        copy.start()
    clear_pads(fields, 5)
    for copy in copies:
        copy.wait()
    square_speed(speed)
    ids = lane_ids()
    for step in range(STEPS):
        moment = STEPS - step
        leap(fields, speed, lanes, step + 1, 4 * (STEPS - 1 - step))
        for shot in range(SHOTS_HERE):

            @pl.loop(0, counts[shot])
            def _(group, shot=shot):
                for member in range(4):
                    item = group * 4 + member
                    row = rows[shot, item]
                    value = misfit[shot * STEPS + moment - 1, index[shot, item]]
                    depth = PAD + (row & (NZ - 1))
                    view = fields.at[step + 2, shot, row >> 5, pl.ds(depth, 1), :]
                    view[...] = view[...] + jnp.where(ids == lanes_of[shot, item], value, 0.0)

    for copy in late:
        copy.wait()

    @pl.loop(0, SLAB)
    def _(plane):
        total = jnp.zeros((NZ, NY), jnp.float32)
        for shot in range(SHOTS_HERE):
            for step in range(STEPS):
                total = total + (
                    fields[step + 2, shot, DEEP + plane, PAD : PAD + NZ, :]
                    * laps[STEPS - 1 - step, shot, plane]
                )
        grad[pl.ds(plane * NZ, NZ), :] = (2.0 * COURANT) * plain[plane] * total

    pack(grad, tiles)


def pack(source, tiles):
    for group in range(NZ // 4):
        block = jnp.concatenate(
            [source[pl.ds(group * 4 + place, SLAB, stride=NZ), :] for place in range(4)], axis=0
        )
        tiles[:, group] = block.T.reshape(tiles.shape[0], 2, 8, NY)


def noise_kernel(noise, tiles, scratch):
    shot = lax.axis_index("shot")
    for group in range(NZ // 4):
        block = jnp.concatenate(
            [noise[pl.ds(group * 4 + place, SLAB, stride=NZ), :] for place in range(4)], axis=0
        )
        scratch[...] = block.T
        tiles[group] = scratch[pl.ds(pl.multiple_of(shot * 16, 16), 16), :].reshape(2, 8, NY)


def swap_blocks(tiles):
    lane = lax.broadcasted_iota(jnp.int32, (8, NY), 1) // SLAB
    swapped = []
    for b in range(4):
        value = tiles[b]
        for a in range(4):
            if a != b:
                value = jnp.where(lane == a, pltpu.roll(tiles[a], (SLAB * (a - b)) % NY, 1), value)
        swapped.append(value)
    return swapped


def gathered(tiles):
    parts = [swap_blocks(tiles[4 * part : 4 * part + 4]) for part in range(4)]
    return jnp.concatenate(
        [jnp.concatenate([parts[part][z] for part in range(4)], axis=1) for z in range(4)], axis=0
    )


def precise(values, high, low):
    first, second = split(values)
    count = values.shape[0]
    both = dot(jnp.concatenate([first, second], axis=0), high)
    return both[:count] + both[count:] + dot(first, low)


def prior_kernel(scales, received, noise, operators, tiles):
    count = received.shape[0] // 16
    sums = []
    for block in range(16):
        total = received[block]
        for shot in range(1, count):
            total = total + received[shot * 16 + block]
        sums.append(total)
    update = scales[0] * precise(gathered(sums), operators[0], operators[1])
    noises = gathered([noise[block] for block in range(16)])
    update = update + scales[1] * precise(noises, operators[2], operators[3])
    for part in range(4):
        lanes = slice(part * NY, (part + 1) * NY)
        swapped = swap_blocks([update[8 * z : 8 * z + 8, lanes] for z in range(4)])
        for place in range(4):
            tiles[4 * part + place] = swapped[place]


def finish_kernel(returned, velocity, out):
    shift = (NY - lax.axis_index("shot") * 16) & (NY - 1)
    for group in range(NZ // 4):
        block = jnp.concatenate([returned[2 * group], returned[2 * group + 1]], axis=0)
        turned = jnp.concatenate([block, jnp.zeros((NY - 16, NY), jnp.float32)], axis=0).T
        for place in range(4):
            where = pl.ds(group * 4 + place, SLAB, stride=NZ)
            base = pltpu.roll(velocity[where, :], shift, 1)
            value = base + turned[place * SLAB : (place + 1) * SLAB]
            out[where, :] = value[:, :16]


def shape(*dims, dtype=jnp.float32):
    return jax.ShapeDtypeStruct(dims, dtype)


def params():
    return pltpu.CompilerParams(vmem_limit_bytes=VMEM_LIMIT)


def neighbours(axis):
    count = lax.axis_size(axis)
    up = [(i, i + 1) for i in range(count - 1)]
    return up, [(b, a) for a, b in up]


def exchange(axis, to_high, to_low):
    up, down = neighbours(axis)
    return lax.ppermute(to_high, axis, up), lax.ppermute(to_low, axis, down)


def edge(deep, shallow, velocity=None):
    both = []
    for begin_deep, begin_shallow in ((SLAB - DEEP, SLAB - SHALLOW), (0, 0)):
        pieces = [deep[s, begin_deep : begin_deep + DEEP] for s in range(SHOTS_HERE)]
        pieces += [shallow[s, begin_shallow : begin_shallow + SHALLOW] for s in range(SHOTS_HERE)]
        if velocity is not None:
            pieces.append(velocity[begin_shallow : begin_shallow + SHALLOW])
        both.append(jnp.concatenate(pieces, axis=0))
    return both


def body(
    velocity,
    noise_field,
    step_size,
    field_prev,
    field_now,
    adjoint_next,
    adjoint_now,
    wavelet,
    source_cells,
    source_signs,
    record_cells,
    observed,
):
    lanes = jnp.asarray(lane_operator())
    operators = jnp.asarray(prior_operators())
    low, high = exchange("dom", *edge(field_now, field_prev, velocity))
    adj_low, adj_high = exchange("dom", *edge(adjoint_now, adjoint_next))

    noise_tiles = pl.pallas_call(
        noise_kernel,
        out_shape=shape(8, 2, 8, NY),
        in_specs=[VMEM],
        out_specs=VMEM,
        scratch_shapes=[pltpu.VMEM((NY, NY), jnp.float32)],
        name="noise_pack",
    )(noise_field.reshape(SLAB * NZ, NY))
    noise_cols = lax.all_to_all(noise_tiles.reshape(16, 8, NY), "dom", 0, 0, tiled=True)

    lists = pl.pallas_call(
        prepare_kernel,
        out_shape=(
            shape(SHOTS_HERE, LIST, dtype=jnp.int32),
            shape(SHOTS_HERE, LIST, dtype=jnp.int32),
            shape(SHOTS_HERE, LIST, dtype=jnp.int32),
            shape(SHOTS_HERE, dtype=jnp.int32),
        ),
        in_specs=[SMEM],
        out_specs=(SMEM,) * 4,
        name="record_lists",
    )(record_cells)

    fields = pltpu.VMEM((STEPS + 2, SHOTS_HERE, ROWS, DEPTH, NY), jnp.float32)
    laplacians, samples = pl.pallas_call(
        forward_kernel,
        out_shape=(shape(STEPS, SHOTS_HERE, SLAB, NZ, NY), shape(SHOTS_HERE * STEPS, NREC)),
        in_specs=[SMEM] * 7 + [ANY] * 5 + [VMEM],
        out_specs=(ANY, VMEM),
        scratch_shapes=[
            fields,
            pltpu.VMEM((STEPS, SHOTS_HERE, ROWS, NZ, NY), jnp.float32),
            pltpu.VMEM((ROWS, NZ, NY), jnp.float32),
            pltpu.SemaphoreType.DMA((15,)),
            pltpu.SemaphoreType.DMA((STEPS,)),
        ],
        compiler_params=params(),
        name="forward_steps",
    )(*lists, source_cells, source_signs, wavelet, field_now, field_prev, velocity, low, high, lanes)

    from_low, from_high = exchange("dom", samples, samples)
    misfit = samples + from_low + from_high - observed.reshape(SHOTS_HERE * STEPS, NREC)

    tiles = pl.pallas_call(
        adjoint_kernel,
        out_shape=shape(8, 8, 2, 8, NY),
        in_specs=[SMEM] * 5 + [ANY] * 8 + [VMEM],
        out_specs=VMEM,
        scratch_shapes=[
            fields,
            pltpu.VMEM((STEPS, SHOTS_HERE, SLAB, NZ, NY), jnp.float32),
            pltpu.VMEM((ROWS, NZ, NY), jnp.float32),
            pltpu.VMEM((SLAB, NZ, NY), jnp.float32),
            pltpu.VMEM((SLAB * NZ, NY), jnp.float32),
            pltpu.SemaphoreType.DMA((17,)),
        ],
        compiler_params=params(),
        name="adjoint_steps",
    )(*lists, misfit, adjoint_now, adjoint_next, velocity, adj_low, adj_high, low, high, laplacians, lanes)

    received = lax.all_to_all(tiles.reshape(128, 8, NY), ("shot", "dom"), 0, 0, tiled=True)
    scales = jnp.concatenate([-0.5 * step_size, jnp.sqrt(step_size)])
    update = pl.pallas_call(
        prior_kernel,
        out_shape=shape(16, 8, NY),
        in_specs=[SMEM, VMEM, VMEM, VMEM],
        out_specs=VMEM,
        compiler_params=params(),
        name="prior",
    )(scales, received, noise_cols, operators)
    returned = lax.all_to_all(update, "dom", 0, 0, tiled=True)
    out = pl.pallas_call(
        finish_kernel,
        out_shape=shape(SLAB * NZ, 16),
        in_specs=[VMEM, VMEM],
        out_specs=VMEM,
        name="finish",
    )(returned, velocity.reshape(SLAB * NZ, NY))
    return out.reshape(SLAB, NZ, 16)


def solution(mesh):
    placed = (
        P("dom", None, None),
        P("dom", None, None),
        P(),
        P("shot", "dom", None, None),
        P("shot", "dom", None, None),
        P("shot", "dom", None, None),
        P("shot", "dom", None, None),
        P("shot", None),
        P("shot", None),
        P("shot", None),
        P("shot", None),
        P("shot", None, None),
    )
    return jax.shard_map(
        body, mesh=mesh, in_specs=placed, out_specs=P("dom", None, "shot"), check_vma=False
    )
```

```python
import math

import jax
import jax.numpy as jnp
import ml_dtypes
import numpy as np
from jax import lax
from jax.experimental import pallas as pl
from jax.experimental.pallas import tpu as pltpu
from jax.sharding import PartitionSpec as P

STEPS = 4
COEFFS = (-205.0 / 72.0, 8.0 / 5.0, -1.0 / 5.0, 8.0 / 315.0, -1.0 / 560.0)
COURANT = 0.02
CUTOFF = 16

NX, NZ, NY = 512, 32, 128
SLAB = 32
DEEP = 16
SHALLOW = 12
ROWS = SLAB + 2 * DEEP
PAD = 8
DEPTH = NZ + 2 * PAD
SHOTS_HERE = 2
NREC = 256
LIST = NREC + 8
CHUNK = 4
VMEM_LIMIT = 56 * 1024 * 1024

ANY = pl.BlockSpec(memory_space=pl.ANY)
VMEM = pl.BlockSpec(memory_space=pltpu.VMEM)
SMEM = pl.BlockSpec(memory_space=pltpu.SMEM)


def split_host(matrix):
    high = matrix.astype(ml_dtypes.bfloat16)
    low = (matrix - high.astype(np.float64)).astype(ml_dtypes.bfloat16)
    return high, low


def lane_operator():
    band = np.zeros((NY, NY))
    np.fill_diagonal(band, 3.0 * COEFFS[0])
    for distance in range(1, 5):
        band += COEFFS[distance] * (np.eye(NY, k=distance) + np.eye(NY, k=-distance))
    high, low = split_host(band)
    zero = np.zeros_like(low)
    return np.block([[high, low], [high, zero]])


def prior_operators():
    wave = np.arange(NX)[:, None]
    position = np.arange(NX)[None, :]
    factor = np.where(wave == 0, math.sqrt(1.0 / NX), math.sqrt(2.0 / NX))
    basis = factor * np.cos(math.pi / (2.0 * NX) * (wave * (2 * position + 1) % (4 * NX)))
    gain = 1.0 / np.sqrt(1.0 + np.arange(NX) / CUTOFF)
    order = np.arange(NX).reshape(NX // 4, 4).T.reshape(-1)
    both = []
    for weight in (gain**2, gain):
        operator = basis.T @ (weight[:, None] * basis)
        both.append(np.stack(split_host(operator[order][:, order])))
    return both


def split(values):
    high = values.astype(jnp.bfloat16)
    low = (values - high.astype(jnp.float32)).astype(jnp.bfloat16)
    return high, low


def dot(left, right):
    return jnp.dot(left, right, preferred_element_type=jnp.float32)


def edge_pairs(deep, shallow, velocity, up, down):
    pairs = []
    for target, deep_at, shallow_at in ((up, SLAB - DEEP, SLAB - SHALLOW), (down, 0, 0)):
        for shot in range(SHOTS_HERE):
            pairs.append((deep.at[shot, pl.ds(deep_at, DEEP)], target.at[pl.ds(shot * DEEP, DEEP)]))
            begin = SHOTS_HERE * DEEP + shot * SHALLOW
            pairs.append((shallow.at[shot, pl.ds(shallow_at, SHALLOW)], target.at[pl.ds(begin, SHALLOW)]))
        if velocity is not None:
            begin = SHOTS_HERE * (DEEP + SHALLOW)
            pairs.append((velocity.at[pl.ds(shallow_at, SHALLOW)], target.at[pl.ds(begin, SHALLOW)]))
    return pairs


def started(pairs, sems):
    copies = [pltpu.make_async_copy(source, target, sems.at[n]) for n, (source, target) in enumerate(pairs)]
    for copy in copies:
        copy.start()
    return copies


def edge_kernel(deep, shallow, velocity, up, down, sems):
    for copy in started(edge_pairs(deep, shallow, velocity, up, down), sems):
        copy.wait()


def prepare_kernel(
    rec, src, deep, shallow, noise, velocity,
    up, down, noise_out, velocity_out, entries, counts, src_entries, src_counts,
    turned, sems,
):
    copies = started(edge_pairs(deep, shallow, None, up, down), sems)
    list_cells(rec, entries, counts)
    list_cells(src, src_entries, src_counts)
    column_slices(noise, noise_out, turned)
    column_slices(velocity, velocity_out, turned)
    for copy in copies:
        copy.wait()


def list_cells(cells, entries, count_out):
    base = (lax.axis_index("dom") * SLAB - SHALLOW) * (NZ * NY)
    span = (SLAB + 2 * SHALLOW) * NZ * NY

    def gather(item, counts):
        following = []
        for shot in range(SHOTS_HERE):
            cell = cells[shot, item] - base
            entries[shot, counts[shot]] = (cell << 8) | item
            inside = (cell >= 0) & (cell < span)
            following.append(counts[shot] + inside.astype(jnp.int32))
        return tuple(following)

    counts = lax.fori_loop(0, cells.shape[1], gather, (jnp.int32(0),) * SHOTS_HERE, unroll=8)
    for shot in range(SHOTS_HERE):
        for extra in range(4):
            entries[shot, counts[shot] + extra] = -1
        count_out[shot] = counts[shot]


def unpack_entry(entry):
    filler = entry < 0
    cell = jnp.where(filler, 0, entry >> 8)
    plane = (cell >> 12) + (DEEP - SHALLOW)
    depth = PAD + ((cell >> 7) & (NZ - 1))
    lane = jnp.where(filler, -1, cell & (NY - 1))
    return plane, depth, lane, jnp.where(filler, 0, entry & (NREC - 1))


def clear_pads(fields):
    zeros = jnp.zeros((ROWS, PAD, NY), jnp.float32)
    for field in fields:
        for shot in range(SHOTS_HERE):
            field[shot, :, 0:PAD, :] = zeros
            field[shot, :, PAD + NZ : DEPTH, :] = zeros


def load_field(field, own, low, high, offset, width, sems, base):
    copies = []
    begin = DEEP - width
    for shot in range(SHOTS_HERE):
        planes = pl.ds(offset + shot * width, width)
        view = field.at[shot]
        for number, (source, target) in enumerate(
            (
                (low.at[planes], view.at[pl.ds(begin, width), pl.ds(PAD, NZ), :]),
                (own.at[shot], view.at[pl.ds(DEEP, SLAB), pl.ds(PAD, NZ), :]),
                (high.at[planes], view.at[pl.ds(DEEP + SLAB, width), pl.ds(PAD, NZ), :]),
            )
        ):
            copies.append(pltpu.make_async_copy(source, target, sems.at[base + shot * 3 + number]))
    return copies


def load_speed(speed, own, low, high, offset, sems, base):
    planes = pl.ds(offset, SHALLOW)
    return [
        pltpu.make_async_copy(low.at[planes], speed.at[pl.ds(DEEP - SHALLOW, SHALLOW)], sems.at[base]),
        pltpu.make_async_copy(own, speed.at[pl.ds(DEEP, SLAB)], sems.at[base + 1]),
        pltpu.make_async_copy(high.at[planes], speed.at[pl.ds(DEEP + SLAB, SHALLOW)], sems.at[base + 2]),
    ]


def square_speed(speed):
    @pl.loop(0, (SLAB + 2 * SHALLOW) // 8)
    def _(part):
        rows = pl.ds(DEEP - SHALLOW + part * 8, 8)
        value = speed[rows]
        speed[rows] = COURANT * value * value


def along_lanes(field, lanes, along, margin):
    first, count = DEEP - margin, SLAB + 2 * margin
    part = count // 2
    for shot in range(SHOTS_HERE):
        for half in range(2):
            begin = first + half * part
            block = field[shot, begin : begin + part, PAD : PAD + NZ, :].reshape(part * NZ, NY)
            both = dot(jnp.concatenate(split(block), axis=1), lanes[...])
            along[shot, begin : begin + part] = (both[:, :NY] + both[:, NY:]).reshape(part, NZ, NY)


def leap(field, before, after, speed, along, margin, laplacians=None, slot=None):
    first = DEEP - margin

    @pl.loop(0, (SLAB + 2 * margin) // CHUNK)
    def _(chunk):
        for plane in range(CHUNK):
            here = first + chunk * CHUNK + plane
            for shot in range(SHOTS_HERE):
                spread = along[shot, here]
                for distance in range(1, 5):
                    beside = (
                        field[shot, here + distance, PAD : PAD + NZ, :]
                        + field[shot, here - distance, PAD : PAD + NZ, :]
                    ) + (
                        field[shot, here, PAD + distance : PAD + NZ + distance, :]
                        + field[shot, here, PAD - distance : PAD + NZ - distance, :]
                    )
                    spread = spread + COEFFS[distance] * beside
                centre = field[shot, here, PAD : PAD + NZ, :]
                after[shot, here, PAD : PAD + NZ, :] = (
                    2.0 * centre - before[shot, here, PAD : PAD + NZ, :] + speed[here] * spread
                )
                if laplacians is not None:
                    laplacians[slot, shot, here] = spread


def lane_ids():
    return lax.broadcasted_iota(jnp.int32, (1, NY), 1)


def forward_kernel(
    entries, counts, src, src_counts, signs, wave,
    now, prev, vel, low, high, lanes, noise,
    lap_out, outgoing,
    *scratch,
):
    fields = scratch[: STEPS + 2]
    laps, speed, along, samples, sems, out_sems = scratch[STEPS + 2 :]
    first_copies = load_field(fields[1], now, low, high, 0, DEEP, sems, 0)
    copies = load_field(fields[0], prev, low, high, 2 * DEEP, SHALLOW, sems, 6)
    copies += load_speed(speed, vel, low, high, 2 * DEEP + 2 * SHALLOW, sems, 12)
    for copy in first_copies + copies:
        copy.start()
    clear_pads(fields[1 : STEPS + 1])
    for copy in first_copies:
        copy.wait()
    ids = lane_ids()
    outs = []
    for moment in range(STEPS):
        margin = 4 * (STEPS - 1 - moment)
        along_lanes(fields[moment + 1], lanes, along, margin)
        if moment == 0:
            for copy in copies:
                copy.wait()
            square_speed(speed)
        leap(fields[moment + 1], fields[moment], fields[moment + 2], speed, along, margin, laps, moment)
        out = pltpu.make_async_copy(laps.at[moment, :, pl.ds(DEEP, SLAB)], lap_out.at[moment], out_sems.at[moment])
        out.start()
        outs.append(out)
        for shot in range(SHOTS_HERE):

            @pl.loop(0, src_counts[shot])
            def _(item, shot=shot):
                plane, depth, lane, which = unpack_entry(src[shot, item])
                amplitude = (2 * signs[shot, which] - 1).astype(jnp.float32) * wave[shot, moment]
                view = fields[moment + 2].at[shot, plane, pl.ds(depth, 1), :]
                view[...] = view[...] + jnp.where(ids == lane, amplitude, 0.0)

    for shot in range(SHOTS_HERE):

        def sample(group, state, shot=shot):
            state = list(state)
            for member in range(4):
                plane, depth, lane, which = unpack_entry(entries[shot, group * 4 + member])
                own = (lane >= 0) & (plane >= DEEP) & (plane < DEEP + SLAB)
                shift = (which - lane) & (NY - 1)
                hits = [ids == jnp.where(own, which - half * NY, -1) for half in range(2)]
                for moment in range(STEPS):
                    line = fields[moment + 2][shot, plane, pl.ds(depth, 1), :]
                    line = pltpu.roll(line, shift, 1)
                    for half in range(2):
                        at = moment * 2 + half
                        state[at] = jnp.where(hits[half], line, state[at])
            return tuple(state)

        zero = jnp.zeros((1, NY), jnp.float32)
        state = lax.fori_loop(0, (counts[shot] + 3) >> 2, sample, (zero,) * (2 * STEPS))
        for moment in range(STEPS):
            for half in range(2):
                line = half * 8 + shot * STEPS + moment
                samples[line : line + 1, :] = state[moment * 2 + half]
    block = samples[...]
    for target in range(16):
        outgoing[target * 24 : target * 24 + 8, :] = noise[target * 8 : target * 8 + 8, :]
        outgoing[target * 24 + 8 : target * 24 + 24, :] = block
    for out in outs:
        out.wait()


def adjoint_kernel(
    entries, counts,
    now, after, vel, low, high, vel_low, vel_high, laps_in, lanes, incoming, observed,
    tiles,
    *scratch,
):
    fields = scratch[: STEPS + 2]
    laps, speed, along, plain, differences, misfit, sems = scratch[STEPS + 2 :]
    first_copies = load_field(fields[1], now, low, high, 0, DEEP, sems, 0)
    copies = load_field(fields[0], after, low, high, 2 * DEEP, SHALLOW, sems, 6)
    copies += load_speed(speed, vel, vel_low, vel_high, 2 * DEEP + 2 * SHALLOW, sems, 12)
    late = [
        pltpu.make_async_copy(laps_in, laps, sems.at[15]),
        pltpu.make_async_copy(vel, plain, sems.at[16]),
    ]
    for copy in first_copies + copies + late:
        copy.start()
    total = incoming[8:24, :]
    for block in range(1, 16):
        total = total + incoming[block * 24 + 8 : block * 24 + 24, :]
    for shot in range(SHOTS_HERE):
        rows = slice(shot * STEPS, (shot + 1) * STEPS)
        for half in range(2):
            columns = slice(half * NY, (half + 1) * NY)
            differences[rows, columns] = (
                total[half * 8 + shot * STEPS : half * 8 + (shot + 1) * STEPS] - observed[shot, :, columns]
            )
    to_scalars = pltpu.make_async_copy(differences, misfit, sems.at[17])
    to_scalars.start()
    clear_pads(fields[1 : STEPS + 1])
    for copy in first_copies:
        copy.wait()
    ids = lane_ids()
    for step in range(STEPS):
        moment = STEPS - step
        margin = 4 * (STEPS - 1 - step)
        along_lanes(fields[step + 1], lanes, along, margin)
        if step == 0:
            for copy in copies:
                copy.wait()
            square_speed(speed)
        leap(fields[step + 1], fields[step], fields[step + 2], speed, along, margin)
        if step == 0:
            to_scalars.wait()
        for shot in range(SHOTS_HERE):

            @pl.loop(0, (counts[shot] + 3) >> 2)
            def _(group, shot=shot):
                for member in range(4):
                    plane, depth, lane, which = unpack_entry(entries[shot, group * 4 + member])
                    value = misfit[shot * STEPS + moment - 1, which]
                    view = fields[step + 2].at[shot, plane, pl.ds(depth, 1), :]
                    view[...] = view[...] + jnp.where(ids == lane, value, 0.0)

    for copy in late:
        copy.wait()
    for group in range(SLAB // 4):
        planes = []
        for plane in range(group * 4, group * 4 + 4):
            total = jnp.zeros((NZ, NY), jnp.float32)
            for shot in range(SHOTS_HERE):
                for step in range(STEPS):
                    total = total + (
                        fields[step + 2][shot, DEEP + plane, PAD : PAD + NZ, :]
                        * laps[STEPS - 1 - step, shot, plane]
                    )
            planes.append((2.0 * COURANT) * plain[plane] * total)
        tiles[pl.ds(group, NY, stride=SLAB // 4), :] = jnp.concatenate(planes, axis=0).T


def column_slices(source, target, turned):
    begin = pl.multiple_of(lax.axis_index("shot") * 16, 16)
    for group in range(SLAB // 4):
        turned[...] = source[group * NY : (group + 1) * NY, :].T
        target[pl.ds(group, 16, stride=SLAB // 4), :] = turned[pl.ds(begin, 16), :]


def apply_prior(columns, operators):
    lane = lax.broadcasted_iota(jnp.int32, (NY, NY), 1)
    blocks = []
    for place in range(4):
        turned = columns if place == 0 else pltpu.roll(columns, NY - 32 * place, 1)
        high = turned.astype(jnp.bfloat16).astype(jnp.float32)
        low = pltpu.roll(turned - high, 32, 1)
        blocks.append(jnp.where(lane < 32, high, low).astype(jnp.bfloat16))
    right = jnp.concatenate(blocks, axis=0)
    upper = dot(operators[0], right)
    lower = dot(operators[1], right)
    result = jnp.zeros((NY, NY), jnp.float32)
    for place in range(4):
        rows = slice(place * NY, (place + 1) * NY)
        value = (upper[rows] + lower[rows]) + pltpu.roll(upper[rows], NY - 32, 1)
        value = pltpu.roll(value, 32 * place, 1) if place else value
        result = jnp.where(lane // 32 == place, value, result)
    return result


def noise_kernel(step_size, incoming, operators, out):
    columns = jnp.concatenate([incoming[block * 24 : block * 24 + 8, :] for block in range(16)], axis=0)
    scale = jnp.sqrt(jnp.full((8, NY), step_size[0], jnp.float32))[0:1]
    out[...] = scale * apply_prior(columns, operators)


def prior_kernel(step_size, received, noise, operators_in, out, parts, operators, sems):
    count = parts.shape[0]
    pairs = [(received.at[pl.ds(part * NY, NY)], parts.at[part]) for part in range(count)]
    copies = started([*pairs, (operators_in, operators)], sems)
    total = None
    for part in range(count):
        copies[part].wait()
        total = parts[part] if part == 0 else total + parts[part]
    copies[count].wait()
    out[...] = (-0.5 * step_size[0]) * apply_prior(total, operators) + noise[...]


def finish_kernel(returned, velocity, out):
    for group in range(SLAB // 4):
        rows = pl.ds(group, 16, stride=SLAB // 4)
        value = returned[rows, :] + velocity[rows, :]
        for place in range(4):
            turned = value if place == 0 else pltpu.roll(value, NY - 32 * place, 1)
            out[group * 4 + place] = turned[:, :NZ]


def shape(*dims, dtype=jnp.float32):
    return jax.ShapeDtypeStruct(dims, dtype)


def params():
    return pltpu.CompilerParams(vmem_limit_bytes=VMEM_LIMIT)


def neighbours(axis):
    count = lax.axis_size(axis)
    up = [(i, i + 1) for i in range(count - 1)]
    return up, [(b, a) for a, b in up]


def exchange(axis, to_high, to_low):
    up, down = neighbours(axis)
    return lax.ppermute(to_high, axis, up), lax.ppermute(to_low, axis, down)


def body(
    velocity,
    noise_field,
    step_size,
    field_prev,
    field_now,
    adjoint_next,
    adjoint_now,
    wavelet,
    source_cells,
    source_signs,
    record_cells,
    observed,
):
    lanes = jnp.asarray(lane_operator())
    squared, single = (jnp.asarray(operator) for operator in prior_operators())
    planes = SHOTS_HERE * (DEEP + SHALLOW)
    up, down = pl.pallas_call(
        edge_kernel,
        out_shape=(shape(planes + SHALLOW, NZ, NY),) * 2,
        in_specs=[ANY] * 3,
        out_specs=(VMEM,) * 2,
        scratch_shapes=[pltpu.SemaphoreType.DMA((10,))],
        name="edges",
    )(field_now, field_prev, velocity)
    low, high = exchange("dom", up, down)
    adjoint_edge, up, down = lax.optimization_barrier((adjoint_now, up, down))

    adj_up, adj_down, noise_tiles, velocity_tiles, *lists = pl.pallas_call(
        prepare_kernel,
        out_shape=(
            *(shape(planes, NZ, NY),) * 2,
            *(shape(NY, NY),) * 2,
            shape(SHOTS_HERE, LIST, dtype=jnp.int32),
            shape(SHOTS_HERE, dtype=jnp.int32),
            shape(SHOTS_HERE, 16, dtype=jnp.int32),
            shape(SHOTS_HERE, dtype=jnp.int32),
        ),
        in_specs=[SMEM] * 2 + [ANY] * 2 + [VMEM] * 2,
        out_specs=(VMEM,) * 4 + (SMEM,) * 4,
        scratch_shapes=[pltpu.VMEM((NY, NY), jnp.float32), pltpu.SemaphoreType.DMA((8,))],
        name="prepare",
    )(
        record_cells, source_cells, adjoint_edge, adjoint_next,
        noise_field.reshape(SLAB * NZ, NY), velocity.reshape(SLAB * NZ, NY),
    )
    adj_low, adj_high = exchange("dom", adj_up, adj_down)

    fields = [pltpu.VMEM((SHOTS_HERE, ROWS, DEPTH, NY), jnp.float32)] * (STEPS + 2)
    speed = pltpu.VMEM((ROWS, NZ, NY), jnp.float32)
    along = pltpu.VMEM((SHOTS_HERE, ROWS, NZ, NY), jnp.float32)
    laplacians, outgoing = pl.pallas_call(
        forward_kernel,
        out_shape=(shape(STEPS, SHOTS_HERE, SLAB, NZ, NY), shape(16 * 24, NY)),
        in_specs=[SMEM] * 6 + [ANY] * 5 + [VMEM] * 2,
        out_specs=(ANY, VMEM),
        scratch_shapes=[
            *fields,
            pltpu.VMEM((STEPS, SHOTS_HERE, ROWS, NZ, NY), jnp.float32),
            speed,
            along,
            pltpu.VMEM((16, NY), jnp.float32),
            pltpu.SemaphoreType.DMA((15,)),
            pltpu.SemaphoreType.DMA((STEPS,)),
        ],
        compiler_params=params(),
        name="forward_steps",
    )(*lists, source_signs, wavelet, field_now, field_prev, velocity, low, high, lanes, noise_tiles)

    incoming = lax.all_to_all(outgoing.reshape(16, 24, NY), "dom", 0, 0, tiled=True).reshape(16 * 24, NY)

    tiles = pl.pallas_call(
        adjoint_kernel,
        out_shape=shape(SLAB * NZ, NY),
        in_specs=[SMEM] * 2 + [ANY] * 8 + [VMEM] * 3,
        out_specs=VMEM,
        scratch_shapes=[
            *fields,
            pltpu.VMEM((STEPS, SHOTS_HERE, SLAB, NZ, NY), jnp.float32),
            speed,
            along,
            pltpu.VMEM((SLAB, NZ, NY), jnp.float32),
            pltpu.VMEM((SHOTS_HERE * STEPS, NREC), jnp.float32),
            pltpu.SMEM((SHOTS_HERE * STEPS, NREC), jnp.float32),
            pltpu.SemaphoreType.DMA((18,)),
        ],
        compiler_params=params(),
        name="adjoint_steps",
    )(
        *lists[:2], adjoint_now, adjoint_next, velocity, adj_low, adj_high, low, high, laplacians,
        lanes, incoming, observed,
    )

    noise_update = pl.pallas_call(
        noise_kernel,
        out_shape=shape(NY, NY),
        in_specs=[SMEM, VMEM, VMEM],
        out_specs=VMEM,
        name="noise_prior",
    )(step_size, incoming, single)

    received = lax.all_to_all(tiles.reshape(128, 8, NY), ("shot", "dom"), 0, 0, tiled=True)
    update = pl.pallas_call(
        prior_kernel,
        out_shape=shape(NY, NY),
        in_specs=[SMEM, ANY, VMEM, ANY],
        out_specs=VMEM,
        scratch_shapes=[
            pltpu.VMEM((8, NY, NY), jnp.float32),
            pltpu.VMEM(squared.shape, jnp.bfloat16),
            pltpu.SemaphoreType.DMA((9,)),
        ],
        name="prior",
    )(step_size, received.reshape(128 * 8, NY), noise_update, squared)
    returned = lax.all_to_all(update.reshape(16, 8, NY), "dom", 0, 0, tiled=True)
    out = pl.pallas_call(
        finish_kernel,
        out_shape=shape(SLAB, 16, NZ),
        in_specs=[VMEM, VMEM],
        out_specs=VMEM,
        name="finish",
    )(returned.reshape(NY, NY), velocity_tiles)
    return out.transpose(0, 2, 1)


def solution(mesh):
    placed = (
        P("dom", None, None),
        P("dom", None, None),
        P(),
        P("shot", "dom", None, None),
        P("shot", "dom", None, None),
        P("shot", "dom", None, None),
        P("shot", "dom", None, None),
        P("shot", None),
        P("shot", None),
        P("shot", None),
        P("shot", None),
        P("shot", None, None),
    )
    return jax.shard_map(
        body, mesh=mesh, in_specs=placed, out_specs=P("dom", None, "shot"), check_vma=False
    )
```

```python
import math

import jax
import jax.numpy as jnp
import ml_dtypes
import numpy as np
from jax import lax
from jax.experimental import pallas as pl
from jax.experimental.pallas import tpu as pltpu
from jax.sharding import PartitionSpec as P

STEPS = 4
COEFFS = (-205.0 / 72.0, 8.0 / 5.0, -1.0 / 5.0, 8.0 / 315.0, -1.0 / 560.0)
COURANT = 0.02
CUTOFF = 16

NX, NZ, NY = 512, 32, 128
SLAB = 32
DEEP = 16
SHALLOW = 12
ROWS = SLAB + 2 * DEEP
PAD = 8
DEPTH = NZ + 2 * PAD
SHOTS_HERE = 2
NREC = 256
LIST = NREC + 8
CHUNK = 4
HALVES = 2
VMEM_LIMIT = 56 * 1024 * 1024

ANY = pl.BlockSpec(memory_space=pl.ANY)
VMEM = pl.BlockSpec(memory_space=pltpu.VMEM)
SMEM = pl.BlockSpec(memory_space=pltpu.SMEM)


def split_host(matrix):
    high = matrix.astype(ml_dtypes.bfloat16)
    low = (matrix - high.astype(np.float64)).astype(ml_dtypes.bfloat16)
    return high, low


def lane_operator():
    band = np.zeros((NY, NY))
    np.fill_diagonal(band, 3.0 * COEFFS[0])
    for distance in range(1, 5):
        band += COEFFS[distance] * (np.eye(NY, k=distance) + np.eye(NY, k=-distance))
    high, low = split_host(band)
    zero = np.zeros_like(low)
    return np.block([[high, low], [high, zero]])


def prior_operators():
    wave = np.arange(NX)[:, None]
    position = np.arange(NX)[None, :]
    factor = np.where(wave == 0, math.sqrt(1.0 / NX), math.sqrt(2.0 / NX))
    basis = factor * np.cos(math.pi / (2.0 * NX) * (wave * (2 * position + 1) % (4 * NX)))
    gain = 1.0 / np.sqrt(1.0 + np.arange(NX) / CUTOFF)
    order = np.arange(NX).reshape(NX // 4, 4).T.reshape(-1)
    both = []
    for weight in (gain**2, gain):
        operator = basis.T @ (weight[:, None] * basis)
        both.append(np.stack(split_host(operator[order][:, order])))
    return both


def split(values):
    high = values.astype(jnp.bfloat16)
    low = (values - high.astype(jnp.float32)).astype(jnp.bfloat16)
    return high, low


def dot(left, right):
    return jnp.dot(left, right, preferred_element_type=jnp.float32)


def edge_pairs(deep, shallow, velocity, up, down):
    pairs = []
    for target, deep_at, shallow_at in ((up, SLAB - DEEP, SLAB - SHALLOW), (down, 0, 0)):
        for shot in range(SHOTS_HERE):
            pairs.append((deep.at[shot, pl.ds(deep_at, DEEP)], target.at[pl.ds(shot * DEEP, DEEP)]))
            begin = SHOTS_HERE * DEEP + shot * SHALLOW
            pairs.append((shallow.at[shot, pl.ds(shallow_at, SHALLOW)], target.at[pl.ds(begin, SHALLOW)]))
        if velocity is not None:
            begin = SHOTS_HERE * (DEEP + SHALLOW)
            pairs.append((velocity.at[pl.ds(shallow_at, SHALLOW)], target.at[pl.ds(begin, SHALLOW)]))
    return pairs


def started(pairs, sems):
    copies = [pltpu.make_async_copy(source, target, sems.at[n]) for n, (source, target) in enumerate(pairs)]
    for copy in copies:
        copy.start()
    return copies


def edge_kernel(deep, shallow, velocity, up, down, sems):
    for copy in started(edge_pairs(deep, shallow, velocity, up, down), sems):
        copy.wait()


def prepare_kernel(
    rec, src, deep, shallow, noise,
    up, down, noise_out, entries, counts, src_entries, src_counts,
    turned, sems,
):
    copies = started(edge_pairs(deep, shallow, None, up, down), sems)
    list_cells(rec, entries, counts)
    list_cells(src, src_entries, src_counts)
    column_slices(noise, noise_out, turned)
    for copy in copies:
        copy.wait()


def list_cells(cells, entries, count_out):
    base = (lax.axis_index("dom") * SLAB - SHALLOW) * (NZ * NY)
    span = (SLAB + 2 * SHALLOW) * NZ * NY

    def gather(item, counts):
        following = []
        for shot in range(SHOTS_HERE):
            cell = cells[shot, item] - base
            entries[shot, counts[shot]] = (cell << 8) | item
            inside = (cell >= 0) & (cell < span)
            following.append(counts[shot] + inside.astype(jnp.int32))
        return tuple(following)

    counts = lax.fori_loop(0, cells.shape[1], gather, (jnp.int32(0),) * SHOTS_HERE, unroll=8)
    for shot in range(SHOTS_HERE):
        for extra in range(4):
            entries[shot, counts[shot] + extra] = -1
        count_out[shot] = counts[shot]


def unpack_entry(entry):
    filler = entry < 0
    cell = jnp.where(filler, 0, entry >> 8)
    plane = (cell >> 12) + (DEEP - SHALLOW)
    depth = PAD + ((cell >> 7) & (NZ - 1))
    lane = jnp.where(filler, -1, cell & (NY - 1))
    return plane, depth, lane, jnp.where(filler, 0, entry & (NREC - 1))


def clear_pads(fields):
    zeros = jnp.zeros((ROWS, PAD, NY), jnp.float32)
    for field in fields:
        for shot in range(SHOTS_HERE):
            field[shot, :, 0:PAD, :] = zeros
            field[shot, :, PAD + NZ : DEPTH, :] = zeros


def own_pairs(field, own):
    return [
        (own.at[shot], field.at[shot, pl.ds(DEEP, SLAB), pl.ds(PAD, NZ), :]) for shot in range(SHOTS_HERE)
    ]


def halo_pairs(field, low, high, offset, width):
    pairs = []
    for shot in range(SHOTS_HERE):
        planes = pl.ds(offset + shot * width, width)
        for source, begin in ((low, DEEP - width), (high, DEEP + SLAB)):
            pairs.append((source.at[planes], field.at[shot, pl.ds(begin, width), pl.ds(PAD, NZ), :]))
    return pairs


def place_halo(field, low, high, offset, width):
    for shot in range(SHOTS_HERE):
        begin = offset + shot * width
        field[shot, DEEP - width : DEEP, PAD : PAD + NZ, :] = low[begin : begin + width]
        field[shot, DEEP + SLAB : DEEP + SLAB + width, PAD : PAD + NZ, :] = high[begin : begin + width]


def square_rows(source, start, target, begin, count):
    for row in range(0, count, 4):
        value = source[start + row : start + row + 4]
        target[begin + row : begin + row + 4] = COURANT * value * value


def along_lanes(field, lanes, along, margin):
    first, count = DEEP - margin, SLAB + 2 * margin
    part = count // HALVES
    for shot in range(SHOTS_HERE):
        for half in range(HALVES):
            begin = first + half * part
            block = field[shot, begin : begin + part, PAD : PAD + NZ, :].reshape(part * NZ, NY)
            both = dot(jnp.concatenate(split(block), axis=1), lanes[...])
            along[shot, begin : begin + part] = (both[:, :NY] + both[:, NY:]).reshape(part, NZ, NY)


def leap(field, before, after, speed, along, margin, laplacians=None, slot=None):
    first = DEEP - margin

    @pl.loop(0, (SLAB + 2 * margin) // CHUNK)
    def _(chunk):
        for plane in range(CHUNK):
            here = first + chunk * CHUNK + plane
            for shot in range(SHOTS_HERE):
                spread = along[shot, here]
                for distance in range(1, 5):
                    beside = (
                        field[shot, here + distance, PAD : PAD + NZ, :]
                        + field[shot, here - distance, PAD : PAD + NZ, :]
                    ) + (
                        field[shot, here, PAD + distance : PAD + NZ + distance, :]
                        + field[shot, here, PAD - distance : PAD + NZ - distance, :]
                    )
                    spread = spread + COEFFS[distance] * beside
                centre = field[shot, here, PAD : PAD + NZ, :]
                after[shot, here, PAD : PAD + NZ, :] = (
                    2.0 * centre - before[shot, here, PAD : PAD + NZ, :] + speed[here] * spread
                )
                if laplacians is not None:
                    laplacians[slot, shot, here] = spread


def lane_ids():
    return lax.broadcasted_iota(jnp.int32, (1, NY), 1)


def forward_kernel(
    entries, counts, src, src_counts, signs, wave,
    now, prev, vel, low, high, lanes, noise,
    lap_out, outgoing, speed_out,
    *scratch,
):
    fields = scratch[: STEPS + 2]
    laps, speed, along, samples, sems, out_sems = scratch[STEPS + 2 :]
    copies = started(
        [
            *own_pairs(fields[1], now),
            (vel, speed.at[pl.ds(DEEP, SLAB)]),
            *own_pairs(fields[0], prev),
        ],
        sems,
    )
    place_halo(fields[1], low, high, 0, DEEP)
    place_halo(fields[0], low, high, SHOTS_HERE * DEEP, SHALLOW)
    begin = SHOTS_HERE * (DEEP + SHALLOW)
    square_rows(low, begin, speed, DEEP - SHALLOW, SHALLOW)
    square_rows(high, begin, speed, DEEP + SLAB, SHALLOW)
    clear_pads(fields[1 : STEPS + 1])
    for copy in copies[:2]:
        copy.wait()
    ids = lane_ids()
    outs = []
    for moment in range(STEPS):
        margin = 4 * (STEPS - 1 - moment)
        along_lanes(fields[moment + 1], lanes, along, margin)
        if moment == 0:
            for copy in copies[2:]:
                copy.wait()
            square_rows(speed, DEEP, speed, DEEP, SLAB)
            outs.append(pltpu.make_async_copy(speed, speed_out, out_sems.at[STEPS]))
            outs[0].start()
        leap(fields[moment + 1], fields[moment], fields[moment + 2], speed, along, margin, laps, moment)
        out = pltpu.make_async_copy(laps.at[moment, :, pl.ds(DEEP, SLAB)], lap_out.at[moment], out_sems.at[moment])
        out.start()
        outs.append(out)
        for shot in range(SHOTS_HERE):

            @pl.loop(0, src_counts[shot])
            def _(item, shot=shot):
                plane, depth, lane, which = unpack_entry(src[shot, item])
                amplitude = (2 * signs[shot, which] - 1).astype(jnp.float32) * wave[shot, moment]
                view = fields[moment + 2].at[shot, plane, pl.ds(depth, 1), :]
                view[...] = view[...] + jnp.where(ids == lane, amplitude, 0.0)

    for shot in range(SHOTS_HERE):

        def sample(group, state, shot=shot):
            state = list(state)
            for member in range(4):
                plane, depth, lane, which = unpack_entry(entries[shot, group * 4 + member])
                own = (lane >= 0) & (plane >= DEEP) & (plane < DEEP + SLAB)
                shift = (which - lane) & (NY - 1)
                hits = [ids == jnp.where(own, which - half * NY, -1) for half in range(2)]
                for moment in range(STEPS):
                    line = fields[moment + 2][shot, plane, pl.ds(depth, 1), :]
                    line = pltpu.roll(line, shift, 1)
                    for half in range(2):
                        at = moment * 2 + half
                        state[at] = jnp.where(hits[half], line, state[at])
            return tuple(state)

        zero = jnp.zeros((1, NY), jnp.float32)
        state = lax.fori_loop(0, (counts[shot] + 3) >> 2, sample, (zero,) * (2 * STEPS))
        for moment in range(STEPS):
            for half in range(2):
                line = half * 8 + shot * STEPS + moment
                samples[line : line + 1, :] = state[moment * 2 + half]
    block = samples[...]
    for target in range(16):
        outgoing[target * 24 : target * 24 + 8, :] = noise[target * 8 : target * 8 + 8, :]
        outgoing[target * 24 + 8 : target * 24 + 24, :] = block
    for out in outs:
        out.wait()


def halo_rows(field):
    pairs = []
    for shot in range(SHOTS_HERE):
        for begin in (DEEP - 8, DEEP + SLAB):
            pairs.append(field.at[shot, pl.ds(begin, 8), pl.ds(PAD, NZ), :])
    return pairs


def adjoint_start_kernel(
    now, after, speed_in, low, high, lanes, earlier_out, halo_out, field, later, earlier, speed, along, sems
):
    copies = started(
        [
            *own_pairs(field, now),
            *halo_pairs(field, low, high, 0, DEEP),
            *own_pairs(later, after),
            *halo_pairs(later, low, high, SHOTS_HERE * DEEP, SHALLOW),
            (speed_in, speed),
        ],
        sems,
    )
    clear_pads([field])
    for copy in copies[:6]:
        copy.wait()
    margin = 4 * (STEPS - 1)
    along_lanes(field, lanes, along, margin)
    for copy in copies[6:]:
        copy.wait()
    outs = started([(rows, halo_out.at[place]) for place, rows in enumerate(halo_rows(field))], sems)
    leap(field, later, earlier, speed, along, margin)
    out = pltpu.make_async_copy(earlier.at[:, :, pl.ds(PAD, NZ), :], earlier_out, sems.at[4])
    out.start()
    for copy in outs:
        copy.wait()
    out.wait()


def adjoint_kernel(
    entries, counts,
    earlier, now, halo, speed_in, vel, laps_in, lanes, incoming, observed,
    tiles,
    *scratch,
):
    fields = [None, *scratch[: STEPS + 1]]
    laps, speed, along, plain, differences, misfit, sems = scratch[STEPS + 1 :]
    copies = started(
        [
            (earlier, fields[2].at[:, :, pl.ds(PAD, NZ), :]),
            *own_pairs(fields[1], now),
            *[(halo.at[place], rows) for place, rows in enumerate(halo_rows(fields[1]))],
            (speed_in, speed),
            (laps_in, laps),
            (vel, plain),
        ],
        sems,
    )
    total = incoming[8:24, :]
    for block in range(1, 16):
        total = total + incoming[block * 24 + 8 : block * 24 + 24, :]
    for shot in range(SHOTS_HERE):
        rows = slice(shot * STEPS, (shot + 1) * STEPS)
        for half in range(2):
            columns = slice(half * NY, (half + 1) * NY)
            differences[rows, columns] = (
                total[half * 8 + shot * STEPS : half * 8 + (shot + 1) * STEPS] - observed[shot, :, columns]
            )
    to_scalars = pltpu.make_async_copy(differences, misfit, sems.at[10])
    to_scalars.start()
    clear_pads(fields[2 : STEPS + 1])
    ids = lane_ids()
    for step in range(STEPS):
        moment = STEPS - step
        if step == 0:
            copies[0].wait()
            to_scalars.wait()
        else:
            margin = 4 * (STEPS - 1 - step)
            along_lanes(fields[step + 1], lanes, along, margin)
            if step == 1:
                for copy in copies[1:8]:
                    copy.wait()
            leap(fields[step + 1], fields[step], fields[step + 2], speed, along, margin)
        for shot in range(SHOTS_HERE):

            @pl.loop(0, (counts[shot] + 3) >> 2)
            def _(group, shot=shot):
                for member in range(4):
                    plane, depth, lane, which = unpack_entry(entries[shot, group * 4 + member])
                    value = misfit[shot * STEPS + moment - 1, which]
                    view = fields[step + 2].at[shot, plane, pl.ds(depth, 1), :]
                    view[...] = view[...] + jnp.where(ids == lane, value, 0.0)

    for copy in copies[8:]:
        copy.wait()
    for group in range(SLAB // 4):
        planes = []
        for plane in range(group * 4, group * 4 + 4):
            total = jnp.zeros((NZ, NY), jnp.float32)
            for shot in range(SHOTS_HERE):
                for step in range(STEPS):
                    total = total + (
                        fields[step + 2][shot, DEEP + plane, PAD : PAD + NZ, :]
                        * laps[STEPS - 1 - step, shot, plane]
                    )
            planes.append((2.0 * COURANT) * plain[plane] * total)
        tiles[pl.ds(group, NY, stride=SLAB // 4), :] = jnp.concatenate(planes, axis=0).T


def column_slices(source, target, turned):
    begin = pl.multiple_of(lax.axis_index("shot") * 16, 16)
    for group in range(SLAB // 4):
        turned[...] = source[group * NY : (group + 1) * NY, :].T
        target[pl.ds(group, 16, stride=SLAB // 4), :] = turned[pl.ds(begin, 16), :]


def apply_prior(columns, operators):
    lane = lax.broadcasted_iota(jnp.int32, (NY, NY), 1)
    blocks = []
    for place in range(4):
        turned = columns if place == 0 else pltpu.roll(columns, NY - 32 * place, 1)
        high = turned.astype(jnp.bfloat16).astype(jnp.float32)
        low = pltpu.roll(turned - high, 32, 1)
        blocks.append(jnp.where(lane < 32, high, low).astype(jnp.bfloat16))
    right = jnp.concatenate(blocks, axis=0)
    upper = dot(operators[0], right)
    lower = dot(operators[1], right)
    result = jnp.zeros((NY, NY), jnp.float32)
    for place in range(4):
        rows = slice(place * NY, (place + 1) * NY)
        value = (upper[rows] + lower[rows]) + pltpu.roll(upper[rows], NY - 32, 1)
        value = pltpu.roll(value, 32 * place, 1) if place else value
        result = jnp.where(lane // 32 == place, value, result)
    return result


def noise_kernel(step_size, incoming, operators, velocity, out, velocity_out, turned):
    column_slices(velocity, velocity_out, turned)
    columns = jnp.concatenate([incoming[block * 24 : block * 24 + 8, :] for block in range(16)], axis=0)
    scale = jnp.sqrt(jnp.full((8, NY), step_size[0], jnp.float32))[0:1]
    out[...] = scale * apply_prior(columns, operators)


def prior_kernel(step_size, received, noise, operators, out):
    total = received[0:NY, :]
    for part in range(1, 8):
        total = total + received[part * NY : (part + 1) * NY, :]
    out[...] = (-0.5 * step_size[0]) * apply_prior(total, operators) + noise[...]


def finish_kernel(returned, velocity, out):
    for group in range(SLAB // 4):
        rows = pl.ds(group, 16, stride=SLAB // 4)
        value = returned[rows, :] + velocity[rows, :]
        for place in range(4):
            turned = value if place == 0 else pltpu.roll(value, NY - 32 * place, 1)
            out[group * 4 + place] = turned[:, :NZ]


def shape(*dims, dtype=jnp.float32):
    return jax.ShapeDtypeStruct(dims, dtype)


def pin(values):
    return pltpu.with_memory_space_constraint(values, pltpu.VMEM)


def leave(*values):
    return [pltpu.with_memory_space_constraint(value, pltpu.HBM) for value in values]


def params():
    return pltpu.CompilerParams(vmem_limit_bytes=VMEM_LIMIT)


def neighbours(axis):
    count = lax.axis_size(axis)
    up = [(i, i + 1) for i in range(count - 1)]
    return up, [(b, a) for a, b in up]


def exchange(axis, to_high, to_low):
    up, down = neighbours(axis)
    return lax.ppermute(to_high, axis, up), lax.ppermute(to_low, axis, down)


def body(
    velocity,
    noise_field,
    step_size,
    field_prev,
    field_now,
    adjoint_next,
    adjoint_now,
    wavelet,
    source_cells,
    source_signs,
    record_cells,
    observed,
):
    lanes = jnp.asarray(lane_operator())
    squared, single = (jnp.asarray(operator) for operator in prior_operators())
    planes = SHOTS_HERE * (DEEP + SHALLOW)
    up, down = pl.pallas_call(
        edge_kernel,
        out_shape=(shape(planes + SHALLOW, NZ, NY),) * 2,
        in_specs=[ANY] * 3,
        out_specs=(VMEM,) * 2,
        scratch_shapes=[pltpu.SemaphoreType.DMA((10,))],
        name="edges",
    )(field_now, field_prev, velocity)
    low, high = exchange("dom", up, down)
    adjoint_edge, up, down = lax.optimization_barrier((adjoint_now, up, down))

    adj_up, adj_down, noise_tiles, *lists = pl.pallas_call(
        prepare_kernel,
        out_shape=(
            *(shape(planes, NZ, NY),) * 2,
            shape(NY, NY),
            shape(SHOTS_HERE, LIST, dtype=jnp.int32),
            shape(SHOTS_HERE, dtype=jnp.int32),
            shape(SHOTS_HERE, 16, dtype=jnp.int32),
            shape(SHOTS_HERE, dtype=jnp.int32),
        ),
        in_specs=[SMEM] * 2 + [ANY] * 2 + [VMEM],
        out_specs=(VMEM,) * 3 + (SMEM,) * 4,
        scratch_shapes=[pltpu.VMEM((NY, NY), jnp.float32), pltpu.SemaphoreType.DMA((8,))],
        name="prepare",
    )(
        record_cells, source_cells, adjoint_edge, adjoint_next,
        noise_field.reshape(SLAB * NZ, NY),
    )
    adj_low, adj_high = exchange("dom", adj_up, adj_down)

    fields = [pltpu.VMEM((SHOTS_HERE, ROWS, DEPTH, NY), jnp.float32)] * (STEPS + 2)
    speed = pltpu.VMEM((ROWS, NZ, NY), jnp.float32)
    along = pltpu.VMEM((SHOTS_HERE, ROWS, NZ, NY), jnp.float32)
    laplacians, outgoing, speed_sq = pl.pallas_call(
        forward_kernel,
        out_shape=(
            shape(STEPS, SHOTS_HERE, SLAB, NZ, NY), shape(16 * 24, NY), shape(ROWS, NZ, NY),
        ),
        in_specs=[SMEM] * 6 + [ANY] * 3 + [VMEM] * 4,
        out_specs=(ANY, VMEM, ANY),
        scratch_shapes=[
            *fields,
            pltpu.VMEM((STEPS, SHOTS_HERE, ROWS, NZ, NY), jnp.float32),
            speed,
            along,
            pltpu.VMEM((16, NY), jnp.float32),
            pltpu.SemaphoreType.DMA((5,)),
            pltpu.SemaphoreType.DMA((STEPS + 1,)),
        ],
        compiler_params=params(),
        name="forward_steps",
    )(
        *leave(*lists, source_signs, wavelet, field_now, field_prev, velocity),
        pin(low), pin(high), *leave(lanes, noise_tiles),
    )

    incoming = lax.all_to_all(outgoing.reshape(16, 24, NY), "dom", 0, 0, tiled=True).reshape(16 * 24, NY)

    field = fields[0]
    earlier, halo = pl.pallas_call(
        adjoint_start_kernel,
        out_shape=(shape(SHOTS_HERE, ROWS, NZ, NY), shape(SHOTS_HERE * 2, 8, NZ, NY)),
        in_specs=[ANY] * 5 + [VMEM],
        out_specs=(ANY,) * 2,
        scratch_shapes=[field, field, field, speed, along, pltpu.SemaphoreType.DMA((13,))],
        compiler_params=params(),
        name="adjoint_start",
    )(*leave(adjoint_now, adjoint_next, speed_sq), pin(adj_low), pin(adj_high), *leave(lanes))
    tiles = pl.pallas_call(
        adjoint_kernel,
        out_shape=shape(SLAB * NZ, NY),
        in_specs=[SMEM] * 2 + [ANY] * 6 + [VMEM] * 3,
        out_specs=VMEM,
        scratch_shapes=[
            *[field] * (STEPS + 1),
            pltpu.VMEM((STEPS, SHOTS_HERE, SLAB, NZ, NY), jnp.float32),
            speed,
            along,
            pltpu.VMEM((SLAB, NZ, NY), jnp.float32),
            pltpu.VMEM((SHOTS_HERE * STEPS, NREC), jnp.float32),
            pltpu.SMEM((SHOTS_HERE * STEPS, NREC), jnp.float32),
            pltpu.SemaphoreType.DMA((11,)),
        ],
        compiler_params=params(),
        name="adjoint_steps",
    )(
        *leave(*lists[:2], earlier, adjoint_now, halo, speed_sq, velocity, laplacians, lanes),
        pin(incoming), *leave(observed),
    )

    noise_update, velocity_tiles = pl.pallas_call(
        noise_kernel,
        out_shape=(shape(NY, NY),) * 2,
        in_specs=[SMEM] + [VMEM] * 3,
        out_specs=(VMEM,) * 2,
        scratch_shapes=[pltpu.VMEM((NY, NY), jnp.float32)],
        name="noise_prior",
    )(step_size, pin(incoming), single, velocity.reshape(SLAB * NZ, NY))

    received = lax.all_to_all(tiles.reshape(128, 8, NY), ("shot", "dom"), 0, 0, tiled=True)
    update = pl.pallas_call(
        prior_kernel,
        out_shape=shape(NY, NY),
        in_specs=[SMEM, VMEM, VMEM, VMEM],
        out_specs=VMEM,
        name="prior",
    )(step_size, pin(received.reshape(128 * 8, NY)), *leave(noise_update), pin(squared))
    returned = lax.all_to_all(update.reshape(16, 8, NY), "dom", 0, 0, tiled=True)
    out = pl.pallas_call(
        finish_kernel,
        out_shape=shape(SLAB, 16, NZ),
        in_specs=[VMEM, VMEM],
        out_specs=VMEM,
        name="finish",
    )(returned.reshape(NY, NY), velocity_tiles)
    return out.transpose(0, 2, 1)


def solution(mesh):
    placed = (
        P("dom", None, None),
        P("dom", None, None),
        P(),
        P("shot", "dom", None, None),
        P("shot", "dom", None, None),
        P("shot", "dom", None, None),
        P("shot", "dom", None, None),
        P("shot", None),
        P("shot", None),
        P("shot", None),
        P("shot", None),
        P("shot", None, None),
    )
    return jax.shard_map(
        body, mesh=mesh, in_specs=placed, out_specs=P("dom", None, "shot"), check_vma=False
    )
```

```python
import math

import jax
import jax.numpy as jnp
import ml_dtypes
import numpy as np
from jax import lax
from jax.experimental import pallas as pl
from jax.experimental.pallas import tpu as pltpu
from jax.sharding import PartitionSpec as P

STEPS = 4
COEFFS = (-205.0 / 72.0, 8.0 / 5.0, -1.0 / 5.0, 8.0 / 315.0, -1.0 / 560.0)
COURANT = 0.02
CUTOFF = 16

NX, NZ, NY = 512, 32, 128
SLAB = 32
DEEP = 16
SHALLOW = 12
ROWS = SLAB + 2 * DEEP
PAD = 8
DEPTH = NZ + 2 * PAD
SHOTS_HERE = 2
NREC = 256
LIST = NREC + 8
CHUNK = 8
HALVES = 1
VMEM_LIMIT = 56 * 1024 * 1024

ANY = pl.BlockSpec(memory_space=pl.ANY)
VMEM = pl.BlockSpec(memory_space=pltpu.VMEM)
SMEM = pl.BlockSpec(memory_space=pltpu.SMEM)


def split_host(matrix):
    high = matrix.astype(ml_dtypes.bfloat16)
    low = (matrix - high.astype(np.float64)).astype(ml_dtypes.bfloat16)
    return high, low


def lane_operator():
    band = np.zeros((NY, NY))
    np.fill_diagonal(band, 3.0 * COEFFS[0])
    for distance in range(1, 5):
        band += COEFFS[distance] * (np.eye(NY, k=distance) + np.eye(NY, k=-distance))
    high, low = split_host(band)
    zero = np.zeros_like(low)
    return np.block([[high, low], [high, zero]])


def prior_operators():
    wave = np.arange(NX)[:, None]
    position = np.arange(NX)[None, :]
    factor = np.where(wave == 0, math.sqrt(1.0 / NX), math.sqrt(2.0 / NX))
    basis = factor * np.cos(math.pi / (2.0 * NX) * (wave * (2 * position + 1) % (4 * NX)))
    gain = 1.0 / np.sqrt(1.0 + np.arange(NX) / CUTOFF)
    order = np.arange(NX).reshape(NX // 4, 4).T.reshape(-1)
    both = []
    for weight in (gain**2, gain):
        operator = basis.T @ (weight[:, None] * basis)
        both.append(np.stack(split_host(operator[order][:, order])))
    return both


def split(values):
    high = values.astype(jnp.bfloat16)
    low = (values - high.astype(jnp.float32)).astype(jnp.bfloat16)
    return high, low


def dot(left, right):
    return jnp.dot(left, right, preferred_element_type=jnp.float32)


def edge_pairs(deep, shallow, velocity, up, down):
    pairs = []
    for target, deep_at, shallow_at in ((up, SLAB - DEEP, SLAB - SHALLOW), (down, 0, 0)):
        for shot in range(SHOTS_HERE):
            pairs.append((deep.at[shot, pl.ds(deep_at, DEEP)], target.at[pl.ds(shot * DEEP, DEEP)]))
            begin = SHOTS_HERE * DEEP + shot * SHALLOW
            pairs.append((shallow.at[shot, pl.ds(shallow_at, SHALLOW)], target.at[pl.ds(begin, SHALLOW)]))
        if velocity is not None:
            begin = SHOTS_HERE * (DEEP + SHALLOW)
            pairs.append((velocity.at[pl.ds(shallow_at, SHALLOW)], target.at[pl.ds(begin, SHALLOW)]))
    return pairs


def started(pairs, sems):
    copies = [pltpu.make_async_copy(source, target, sems.at[n]) for n, (source, target) in enumerate(pairs)]
    for copy in copies:
        copy.start()
    return copies


def stage_edges(deep, shallow, velocity, up, down, staged, sems):
    inward = started(edge_pairs(deep, shallow, velocity, *staged), sems.at[0])
    targets = edge_pairs(deep, shallow, velocity, up, down)
    sources = edge_pairs(deep, shallow, velocity, *staged)
    outward = []
    for number, copy in enumerate(inward):
        copy.wait()
        out = pltpu.make_async_copy(sources[number][1], targets[number][1], sems.at[1, number])
        out.start()
        outward.append(out)
    return outward


def edge_kernel(deep, shallow, velocity, up, down, high, low, sems):
    for copy in stage_edges(deep, shallow, velocity, up, down, (high, low), sems):
        copy.wait()


def prepare_kernel(
    rec, src, deep, shallow, noise,
    up, down, noise_out, entries, counts, src_entries, src_counts,
    turned, high, low, sems,
):
    copies = stage_edges(deep, shallow, None, up, down, (high, low), sems)
    list_cells(rec, entries, counts)
    list_cells(src, src_entries, src_counts)
    column_slices(noise, noise_out, turned)
    for copy in copies:
        copy.wait()


def list_cells(cells, entries, count_out):
    base = (lax.axis_index("dom") * SLAB - SHALLOW) * (NZ * NY)
    span = (SLAB + 2 * SHALLOW) * NZ * NY

    def gather(item, counts):
        following = []
        for shot in range(SHOTS_HERE):
            cell = cells[shot, item] - base
            entries[shot, counts[shot]] = (cell << 8) | item
            inside = (cell >= 0) & (cell < span)
            following.append(counts[shot] + inside.astype(jnp.int32))
        return tuple(following)

    counts = lax.fori_loop(0, cells.shape[1], gather, (jnp.int32(0),) * SHOTS_HERE, unroll=8)
    for shot in range(SHOTS_HERE):
        for extra in range(4):
            entries[shot, counts[shot] + extra] = -1
        count_out[shot] = counts[shot]


def unpack_entry(entry):
    plane = (entry >> 20) + (DEEP - SHALLOW)
    depth = PAD + ((entry >> 15) & (NZ - 1))
    lane = ((entry >> 8) & (NY - 1)) | (entry >> 31)
    return plane, depth, lane, entry & (NREC - 1)


def clear_pads(fields):
    zeros = jnp.zeros((ROWS, PAD, NY), jnp.float32)
    for field in fields:
        for shot in range(SHOTS_HERE):
            field[shot, :, 0:PAD, :] = zeros
            field[shot, :, PAD + NZ : DEPTH, :] = zeros


def own_pairs(field, own):
    return [
        (own.at[shot], field.at[shot, pl.ds(DEEP, SLAB), pl.ds(PAD, NZ), :]) for shot in range(SHOTS_HERE)
    ]


def halo_pairs(field, low, high, offset, width):
    pairs = []
    for shot in range(SHOTS_HERE):
        planes = pl.ds(offset + shot * width, width)
        for source, begin in ((low, DEEP - width), (high, DEEP + SLAB)):
            pairs.append((source.at[planes], field.at[shot, pl.ds(begin, width), pl.ds(PAD, NZ), :]))
    return pairs


def place_halo(field, low, high, offset, width):
    for shot in range(SHOTS_HERE):
        begin = offset + shot * width
        field[shot, DEEP - width : DEEP, PAD : PAD + NZ, :] = low[begin : begin + width]
        field[shot, DEEP + SLAB : DEEP + SLAB + width, PAD : PAD + NZ, :] = high[begin : begin + width]


def square_rows(source, start, target, begin, count):
    for row in range(0, count, 4):
        value = source[start + row : start + row + 4]
        target[begin + row : begin + row + 4] = COURANT * value * value


def along_lanes(field, lanes, along, margin):
    first, count = DEEP - margin, SLAB + 2 * margin
    part = count // HALVES
    for shot in range(SHOTS_HERE):
        for half in range(HALVES):
            begin = first + half * part
            block = field[shot, begin : begin + part, PAD : PAD + NZ, :].reshape(part * NZ, NY)
            both = dot(jnp.concatenate(split(block), axis=1), lanes[...])
            along[shot, begin : begin + part] = (both[:, :NY] + both[:, NY:]).reshape(part, NZ, NY)


def leap(field, before, after, speed, along, margin, laplacians=None, slot=None):
    first = DEEP - margin

    @pl.loop(0, (SLAB + 2 * margin) // CHUNK)
    def _(chunk):
        for plane in range(CHUNK):
            here = first + chunk * CHUNK + plane
            for shot in range(SHOTS_HERE):
                spread = along[shot, here]
                for distance in range(1, 5):
                    beside = (
                        field[shot, here + distance, PAD : PAD + NZ, :]
                        + field[shot, here - distance, PAD : PAD + NZ, :]
                    ) + (
                        field[shot, here, PAD + distance : PAD + NZ + distance, :]
                        + field[shot, here, PAD - distance : PAD + NZ - distance, :]
                    )
                    spread = spread + COEFFS[distance] * beside
                centre = field[shot, here, PAD : PAD + NZ, :]
                after[shot, here, PAD : PAD + NZ, :] = (
                    2.0 * centre - before[shot, here, PAD : PAD + NZ, :] + speed[here] * spread
                )
                if laplacians is not None:
                    laplacians[slot, shot, here] = spread


def lane_ids():
    return lax.broadcasted_iota(jnp.int32, (1, NY), 1)


def forward_kernel(
    entries, counts, src, src_counts, signs, wave,
    now, prev, vel, low, high, lanes, noise,
    lap_out, outgoing, speed_out,
    *scratch,
):
    fields = scratch[: STEPS + 2]
    laps, speed, along, samples, sems, out_sems = scratch[STEPS + 2 :]
    copies = started(
        [
            *own_pairs(fields[1], now),
            (vel, speed.at[pl.ds(DEEP, SLAB)]),
            *own_pairs(fields[0], prev),
        ],
        sems,
    )
    place_halo(fields[1], low, high, 0, DEEP)
    place_halo(fields[0], low, high, SHOTS_HERE * DEEP, SHALLOW)
    begin = SHOTS_HERE * (DEEP + SHALLOW)
    square_rows(low, begin, speed, DEEP - SHALLOW, SHALLOW)
    square_rows(high, begin, speed, DEEP + SLAB, SHALLOW)
    clear_pads(fields[1 : STEPS + 1])
    for copy in copies[:2]:
        copy.wait()
    ids = lane_ids()
    outs = []
    for moment in range(STEPS):
        margin = 4 * (STEPS - 1 - moment)
        along_lanes(fields[moment + 1], lanes, along, margin)
        if moment == 0:
            for copy in copies[2:]:
                copy.wait()
            square_rows(speed, DEEP, speed, DEEP, SLAB)
            outs.append(pltpu.make_async_copy(speed, speed_out, out_sems.at[STEPS]))
            outs[0].start()
        leap(fields[moment + 1], fields[moment], fields[moment + 2], speed, along, margin, laps, moment)
        out = pltpu.make_async_copy(laps.at[moment, :, pl.ds(DEEP, SLAB)], lap_out.at[moment], out_sems.at[moment])
        out.start()
        outs.append(out)
        for shot in range(SHOTS_HERE):

            @pl.loop(0, src_counts[shot])
            def _(item, shot=shot):
                plane, depth, lane, which = unpack_entry(src[shot, item])
                amplitude = (2 * signs[shot, which] - 1).astype(jnp.float32) * wave[shot, moment]
                view = fields[moment + 2].at[shot, plane, pl.ds(depth, 1), :]
                view[...] = view[...] + jnp.where(ids == lane, amplitude, 0.0)

    for shot in range(SHOTS_HERE):

        def sample(group, state, shot=shot):
            state = list(state)
            for member in range(4):
                plane, depth, lane, which = unpack_entry(entries[shot, group * 4 + member])
                own = (lane >= 0) & (plane >= DEEP) & (plane < DEEP + SLAB)
                shift = (which - lane) & (NY - 1)
                hits = [ids == jnp.where(own, which - half * NY, -1) for half in range(2)]
                for moment in range(STEPS):
                    line = fields[moment + 2][shot, plane, pl.ds(depth, 1), :]
                    line = pltpu.roll(line, shift, 1)
                    for half in range(2):
                        at = moment * 2 + half
                        state[at] = jnp.where(hits[half], line, state[at])
            return tuple(state)

        zero = jnp.zeros((1, NY), jnp.float32)
        state = lax.fori_loop(0, (counts[shot] + 3) >> 2, sample, (zero,) * (2 * STEPS))
        for moment in range(STEPS):
            for half in range(2):
                line = half * 8 + shot * STEPS + moment
                samples[line : line + 1, :] = state[moment * 2 + half]
    block = samples[...]
    for target in range(16):
        outgoing[target * 24 : target * 24 + 8, :] = noise[target * 8 : target * 8 + 8, :]
        outgoing[target * 24 + 8 : target * 24 + 24, :] = block
    for out in outs:
        out.wait()


def halo_rows(field):
    pairs = []
    for shot in range(SHOTS_HERE):
        for begin in (DEEP - 8, DEEP + SLAB):
            pairs.append(field.at[shot, pl.ds(begin, 8), pl.ds(PAD, NZ), :])
    return pairs


def adjoint_start_kernel(
    now, after, speed_in, low, high, lanes, earlier_out, halo_out, field, later, earlier, speed, along, sems
):
    copies = started(
        [
            *own_pairs(field, now),
            *halo_pairs(field, low, high, 0, DEEP),
            *own_pairs(later, after),
            *halo_pairs(later, low, high, SHOTS_HERE * DEEP, SHALLOW),
            (speed_in, speed),
        ],
        sems,
    )
    clear_pads([field])
    for copy in copies[:6]:
        copy.wait()
    margin = 4 * (STEPS - 1)
    along_lanes(field, lanes, along, margin)
    for copy in copies[6:]:
        copy.wait()
    outs = started([(rows, halo_out.at[place]) for place, rows in enumerate(halo_rows(field))], sems)
    leap(field, later, earlier, speed, along, margin)
    out = pltpu.make_async_copy(earlier.at[:, :, pl.ds(PAD, NZ), :], earlier_out, sems.at[4])
    out.start()
    for copy in outs:
        copy.wait()
    out.wait()


def adjoint_kernel(
    entries, counts,
    earlier, now, halo, speed_in, vel, laps_in, lanes, incoming, observed,
    tiles,
    *scratch,
):
    fields = [None, *scratch[: STEPS + 1]]
    laps, speed, along, plain, differences, misfit, sems = scratch[STEPS + 1 :]
    copies = started(
        [
            (earlier, fields[2].at[:, :, pl.ds(PAD, NZ), :]),
            *own_pairs(fields[1], now),
            *[(halo.at[place], rows) for place, rows in enumerate(halo_rows(fields[1]))],
            (speed_in, speed),
            (laps_in, laps),
            (vel, plain),
        ],
        sems,
    )
    total = incoming[8:24, :]
    for block in range(1, 16):
        total = total + incoming[block * 24 + 8 : block * 24 + 24, :]
    for shot in range(SHOTS_HERE):
        rows = slice(shot * STEPS, (shot + 1) * STEPS)
        for half in range(2):
            columns = slice(half * NY, (half + 1) * NY)
            differences[rows, columns] = (
                total[half * 8 + shot * STEPS : half * 8 + (shot + 1) * STEPS] - observed[shot, :, columns]
            )
    to_scalars = pltpu.make_async_copy(differences, misfit, sems.at[10])
    to_scalars.start()
    clear_pads(fields[2 : STEPS + 1])
    ids = lane_ids()
    for step in range(STEPS):
        moment = STEPS - step
        if step == 0:
            copies[0].wait()
            to_scalars.wait()
        else:
            margin = 4 * (STEPS - 1 - step)
            along_lanes(fields[step + 1], lanes, along, margin)
            if step == 1:
                for copy in copies[1:8]:
                    copy.wait()
            leap(fields[step + 1], fields[step], fields[step + 2], speed, along, margin)
        for shot in range(SHOTS_HERE):

            @pl.loop(0, (counts[shot] + 3) >> 2)
            def _(group, shot=shot):
                for member in range(4):
                    plane, depth, lane, which = unpack_entry(entries[shot, group * 4 + member])
                    value = misfit[shot * STEPS + moment - 1, which]
                    view = fields[step + 2].at[shot, plane, pl.ds(depth, 1), :]
                    view[...] = view[...] + jnp.where(ids == lane, value, 0.0)

    for copy in copies[8:]:
        copy.wait()
    for group in range(SLAB // 4):
        planes = []
        for plane in range(group * 4, group * 4 + 4):
            total = jnp.zeros((NZ, NY), jnp.float32)
            for shot in range(SHOTS_HERE):
                for step in range(STEPS):
                    total = total + (
                        fields[step + 2][shot, DEEP + plane, PAD : PAD + NZ, :]
                        * laps[STEPS - 1 - step, shot, plane]
                    )
            planes.append((2.0 * COURANT) * plain[plane] * total)
        tiles[pl.ds(group, NY, stride=SLAB // 4), :] = jnp.concatenate(planes, axis=0).T


def column_slices(source, target, turned):
    begin = pl.multiple_of(lax.axis_index("shot") * 16, 16)
    for group in range(SLAB // 4):
        turned[...] = source[group * NY : (group + 1) * NY, :].T
        target[pl.ds(group, 16, stride=SLAB // 4), :] = turned[pl.ds(begin, 16), :]


def apply_prior(columns, operators):
    lane = lax.broadcasted_iota(jnp.int32, (NY, NY), 1)
    blocks = []
    for place in range(4):
        turned = columns if place == 0 else pltpu.roll(columns, NY - 32 * place, 1)
        high = turned.astype(jnp.bfloat16).astype(jnp.float32)
        low = pltpu.roll(turned - high, 32, 1)
        blocks.append(jnp.where(lane < 32, high, low).astype(jnp.bfloat16))
    right = jnp.concatenate(blocks, axis=0)
    upper = dot(operators[0], right)
    lower = dot(operators[1], right)
    result = jnp.zeros((NY, NY), jnp.float32)
    for place in range(4):
        rows = slice(place * NY, (place + 1) * NY)
        value = (upper[rows] + lower[rows]) + pltpu.roll(upper[rows], NY - 32, 1)
        value = pltpu.roll(value, 32 * place, 1) if place else value
        result = jnp.where(lane // 32 == place, value, result)
    return result


def noise_kernel(step_size, incoming, operators, velocity, out, velocity_out, turned):
    column_slices(velocity, velocity_out, turned)
    columns = jnp.concatenate([incoming[block * 24 : block * 24 + 8, :] for block in range(16)], axis=0)
    scale = jnp.sqrt(jnp.full((8, NY), step_size[0], jnp.float32))[0:1]
    out[...] = scale * apply_prior(columns, operators)


def prior_kernel(step_size, received, noise, operators, out):
    total = received[0:NY, :]
    for part in range(1, 8):
        total = total + received[part * NY : (part + 1) * NY, :]
    out[...] = (-0.5 * step_size[0]) * apply_prior(total, operators) + noise[...]


def finish_kernel(returned, velocity, out):
    for group in range(SLAB // 4):
        rows = pl.ds(group, 16, stride=SLAB // 4)
        value = returned[rows, :] + velocity[rows, :]
        for place in range(4):
            turned = value if place == 0 else pltpu.roll(value, NY - 32 * place, 1)
            out[group * 4 + place] = turned[:, :NZ]


def shape(*dims, dtype=jnp.float32):
    return jax.ShapeDtypeStruct(dims, dtype)


def pin(values):
    return pltpu.with_memory_space_constraint(values, pltpu.VMEM)


def leave(*values):
    return [pltpu.with_memory_space_constraint(value, pltpu.HBM) for value in values]


def params():
    return pltpu.CompilerParams(vmem_limit_bytes=VMEM_LIMIT)


def neighbours(axis):
    count = lax.axis_size(axis)
    up = [(i, i + 1) for i in range(count - 1)]
    return up, [(b, a) for a, b in up]


def exchange(axis, to_high, to_low):
    up, down = neighbours(axis)
    return lax.ppermute(to_high, axis, up), lax.ppermute(to_low, axis, down)


def body(
    velocity,
    noise_field,
    step_size,
    field_prev,
    field_now,
    adjoint_next,
    adjoint_now,
    wavelet,
    source_cells,
    source_signs,
    record_cells,
    observed,
):
    lanes = jnp.asarray(lane_operator())
    squared, single = (jnp.asarray(operator) for operator in prior_operators())
    planes = SHOTS_HERE * (DEEP + SHALLOW)
    up, down = pl.pallas_call(
        edge_kernel,
        out_shape=(shape(planes + SHALLOW, NZ, NY),) * 2,
        in_specs=[ANY] * 3,
        out_specs=(ANY,) * 2,
        scratch_shapes=[
            *[pltpu.VMEM((planes + SHALLOW, NZ, NY), jnp.float32)] * 2,
            pltpu.SemaphoreType.DMA((2, 10)),
        ],
        name="edges",
    )(field_now, field_prev, velocity)
    low, high = exchange("dom", up, down)
    adjoint_edge, up, down = lax.optimization_barrier((adjoint_now, up, down))

    adj_up, adj_down, noise_tiles, *lists = pl.pallas_call(
        prepare_kernel,
        out_shape=(
            *(shape(planes, NZ, NY),) * 2,
            shape(NY, NY),
            shape(SHOTS_HERE, LIST, dtype=jnp.int32),
            shape(SHOTS_HERE, dtype=jnp.int32),
            shape(SHOTS_HERE, 16, dtype=jnp.int32),
            shape(SHOTS_HERE, dtype=jnp.int32),
        ),
        in_specs=[SMEM] * 2 + [ANY] * 2 + [VMEM],
        out_specs=(ANY,) * 2 + (VMEM,) + (SMEM,) * 4,
        scratch_shapes=[
            pltpu.VMEM((NY, NY), jnp.float32),
            *[pltpu.VMEM((planes, NZ, NY), jnp.float32)] * 2,
            pltpu.SemaphoreType.DMA((2, 8)),
        ],
        name="prepare",
    )(
        record_cells, source_cells, adjoint_edge, adjoint_next,
        noise_field.reshape(SLAB * NZ, NY),
    )
    adj_low, adj_high = exchange("dom", adj_up, adj_down)

    fields = [pltpu.VMEM((SHOTS_HERE, ROWS, DEPTH, NY), jnp.float32)] * (STEPS + 2)
    speed = pltpu.VMEM((ROWS, NZ, NY), jnp.float32)
    along = pltpu.VMEM((SHOTS_HERE, ROWS, NZ, NY), jnp.float32)
    laplacians, outgoing, speed_sq = pl.pallas_call(
        forward_kernel,
        out_shape=(
            shape(STEPS, SHOTS_HERE, SLAB, NZ, NY), shape(16 * 24, NY), shape(ROWS, NZ, NY),
        ),
        in_specs=[SMEM] * 6 + [ANY] * 3 + [VMEM] * 4,
        out_specs=(ANY, VMEM, ANY),
        scratch_shapes=[
            *fields,
            pltpu.VMEM((STEPS, SHOTS_HERE, ROWS, NZ, NY), jnp.float32),
            speed,
            along,
            pltpu.VMEM((16, NY), jnp.float32),
            pltpu.SemaphoreType.DMA((5,)),
            pltpu.SemaphoreType.DMA((STEPS + 1,)),
        ],
        compiler_params=params(),
        name="forward_steps",
    )(
        *leave(*lists, source_signs, wavelet, field_now, field_prev, velocity),
        pin(low), pin(high), *leave(lanes, noise_tiles),
    )

    incoming = lax.all_to_all(outgoing.reshape(16, 24, NY), "dom", 0, 0, tiled=True).reshape(16 * 24, NY)

    field = fields[0]
    earlier, halo = pl.pallas_call(
        adjoint_start_kernel,
        out_shape=(shape(SHOTS_HERE, ROWS, NZ, NY), shape(SHOTS_HERE * 2, 8, NZ, NY)),
        in_specs=[ANY] * 5 + [VMEM],
        out_specs=(ANY,) * 2,
        scratch_shapes=[field, field, field, speed, along, pltpu.SemaphoreType.DMA((13,))],
        compiler_params=params(),
        name="adjoint_start",
    )(*leave(adjoint_now, adjoint_next, speed_sq), pin(adj_low), pin(adj_high), *leave(lanes))
    tiles = pl.pallas_call(
        adjoint_kernel,
        out_shape=shape(SLAB * NZ, NY),
        in_specs=[SMEM] * 2 + [ANY] * 6 + [VMEM] * 3,
        out_specs=VMEM,
        scratch_shapes=[
            *[field] * (STEPS + 1),
            pltpu.VMEM((STEPS, SHOTS_HERE, SLAB, NZ, NY), jnp.float32),
            speed,
            along,
            pltpu.VMEM((SLAB, NZ, NY), jnp.float32),
            pltpu.VMEM((SHOTS_HERE * STEPS, NREC), jnp.float32),
            pltpu.SMEM((SHOTS_HERE * STEPS, NREC), jnp.float32),
            pltpu.SemaphoreType.DMA((11,)),
        ],
        compiler_params=params(),
        name="adjoint_steps",
    )(
        *leave(*lists[:2], earlier, adjoint_now, halo, speed_sq, velocity, laplacians, lanes),
        pin(incoming), *leave(observed),
    )

    noise_update, velocity_tiles = pl.pallas_call(
        noise_kernel,
        out_shape=(shape(NY, NY),) * 2,
        in_specs=[SMEM] + [VMEM] * 3,
        out_specs=(VMEM,) * 2,
        scratch_shapes=[pltpu.VMEM((NY, NY), jnp.float32)],
        name="noise_prior",
    )(step_size, pin(incoming), single, velocity.reshape(SLAB * NZ, NY))

    received = lax.all_to_all(tiles.reshape(128, 8, NY), ("shot", "dom"), 0, 0, tiled=True)
    update = pl.pallas_call(
        prior_kernel,
        out_shape=shape(NY, NY),
        in_specs=[SMEM, VMEM, VMEM, VMEM],
        out_specs=VMEM,
        name="prior",
    )(step_size, pin(received.reshape(128 * 8, NY)), *leave(noise_update), pin(squared))
    returned = lax.all_to_all(update.reshape(16, 8, NY), "dom", 0, 0, tiled=True)
    out = pl.pallas_call(
        finish_kernel,
        out_shape=shape(SLAB, 16, NZ),
        in_specs=[VMEM, VMEM],
        out_specs=VMEM,
        name="finish",
    )(returned.reshape(NY, NY), velocity_tiles)
    return out.transpose(0, 2, 1)


def solution(mesh):
    placed = (
        P("dom", None, None),
        P("dom", None, None),
        P(),
        P("shot", "dom", None, None),
        P("shot", "dom", None, None),
        P("shot", "dom", None, None),
        P("shot", "dom", None, None),
        P("shot", None),
        P("shot", None),
        P("shot", None),
        P("shot", None),
        P("shot", None, None),
    )
    return jax.shard_map(
        body, mesh=mesh, in_specs=placed, out_specs=P("dom", None, "shot"), check_vma=False
    )
```

```python
import math

import jax
import jax.numpy as jnp
import ml_dtypes
import numpy as np
from jax import lax
from jax.experimental import pallas as pl
from jax.experimental.pallas import tpu as pltpu
from jax.sharding import PartitionSpec as P

STEPS = 4
COEFFS = (-205.0 / 72.0, 8.0 / 5.0, -1.0 / 5.0, 8.0 / 315.0, -1.0 / 560.0)
COURANT = 0.02
CUTOFF = 16

NX, NZ, NY = 512, 32, 128
SLAB = 32
DEEP = 16
SHALLOW = 12
ROWS = SLAB + 2 * DEEP
PAD = 8
DEPTH = NZ + 2 * PAD
SHOTS_HERE = 2
NREC = 256
LIST = NREC + 8
CHUNK = 8
HALVES = 1
VMEM_LIMIT = 56 * 1024 * 1024

ANY = pl.BlockSpec(memory_space=pl.ANY)
VMEM = pl.BlockSpec(memory_space=pltpu.VMEM)
SMEM = pl.BlockSpec(memory_space=pltpu.SMEM)


def split_host(matrix):
    high = matrix.astype(ml_dtypes.bfloat16)
    low = (matrix - high.astype(np.float64)).astype(ml_dtypes.bfloat16)
    return high, low


def lane_operator():
    band = np.zeros((NY, NY))
    np.fill_diagonal(band, 3.0 * COEFFS[0])
    for distance in range(1, 5):
        band += COEFFS[distance] * (np.eye(NY, k=distance) + np.eye(NY, k=-distance))
    high, low = split_host(band)
    zero = np.zeros_like(low)
    return np.block([[high, low], [high, zero]])


def prior_operators():
    wave = np.arange(NX)[:, None]
    position = np.arange(NX)[None, :]
    factor = np.where(wave == 0, math.sqrt(1.0 / NX), math.sqrt(2.0 / NX))
    basis = factor * np.cos(math.pi / (2.0 * NX) * (wave * (2 * position + 1) % (4 * NX)))
    gain = 1.0 / np.sqrt(1.0 + np.arange(NX) / CUTOFF)
    order = np.arange(NX).reshape(NX // 4, 4).T.reshape(-1)
    both = []
    for weight in (gain**2, gain):
        operator = basis.T @ (weight[:, None] * basis)
        both.append(np.stack(split_host(operator[order][:, order])))
    return both


def split(values):
    high = values.astype(jnp.bfloat16)
    low = (values - high.astype(jnp.float32)).astype(jnp.bfloat16)
    return high, low


def dot(left, right):
    return jnp.dot(left, right, preferred_element_type=jnp.float32)


def edge_pairs(deep, shallow, velocity, up, down):
    pairs = []
    for target, deep_at, shallow_at in ((up, SLAB - DEEP, SLAB - SHALLOW), (down, 0, 0)):
        for shot in range(SHOTS_HERE):
            pairs.append((deep.at[shot, pl.ds(deep_at, DEEP)], target.at[pl.ds(shot * DEEP, DEEP)]))
            begin = SHOTS_HERE * DEEP + shot * SHALLOW
            pairs.append((shallow.at[shot, pl.ds(shallow_at, SHALLOW)], target.at[pl.ds(begin, SHALLOW)]))
        if velocity is not None:
            begin = SHOTS_HERE * (DEEP + SHALLOW)
            pairs.append((velocity.at[pl.ds(shallow_at, SHALLOW)], target.at[pl.ds(begin, SHALLOW)]))
    return pairs


def started(pairs, sems):
    copies = [pltpu.make_async_copy(source, target, sems.at[n]) for n, (source, target) in enumerate(pairs)]
    for copy in copies:
        copy.start()
    return copies


def stage_edges(deep, shallow, velocity, up, down, staged, sems):
    inward = started(edge_pairs(deep, shallow, velocity, *staged), sems.at[0])
    targets = edge_pairs(deep, shallow, velocity, up, down)
    sources = edge_pairs(deep, shallow, velocity, *staged)
    outward = []
    for number, copy in enumerate(inward):
        copy.wait()
        out = pltpu.make_async_copy(sources[number][1], targets[number][1], sems.at[1, number])
        out.start()
        outward.append(out)
    return outward


def edge_kernel(deep, shallow, velocity, up, down, high, low, sems):
    for copy in stage_edges(deep, shallow, velocity, up, down, (high, low), sems):
        copy.wait()


def prepare_kernel(
    rec, src, deep, shallow, noise,
    up, down, noise_out, own, own_count, halo, halo_count, src_entries, src_counts,
    turned, high, low, sems,
):
    copies = stage_edges(deep, shallow, None, up, down, (high, low), sems)
    list_receivers(rec, own, own_count, halo, halo_count)
    list_cells(src, src_entries, src_counts)
    column_slices(noise, noise_out, turned)
    for copy in copies:
        copy.wait()


def list_cells(cells, entries, count_out):
    base = (lax.axis_index("dom") * SLAB - SHALLOW) * (NZ * NY)
    span = (SLAB + 2 * SHALLOW) * NZ * NY

    def gather(item, counts):
        following = []
        for shot in range(SHOTS_HERE):
            cell = cells[shot, item] - base
            entries[shot, counts[shot]] = (cell << 8) | item
            inside = (cell >= 0) & (cell < span)
            following.append(counts[shot] + inside.astype(jnp.int32))
        return tuple(following)

    counts = lax.fori_loop(0, cells.shape[1], gather, (jnp.int32(0),) * SHOTS_HERE, unroll=8)
    for shot in range(SHOTS_HERE):
        for extra in range(4):
            entries[shot, counts[shot] + extra] = -1
        count_out[shot] = counts[shot]


def list_receivers(cells, own, own_count, halo, halo_count):
    base = (lax.axis_index("dom") * SLAB - SHALLOW) * (NZ * NY)
    begin, end = SHALLOW * NZ * NY, (SHALLOW + SLAB) * NZ * NY
    span = (SLAB + 2 * SHALLOW) * NZ * NY

    def gather(item, counts):
        following = []
        for shot in range(SHOTS_HERE):
            first, second = counts[2 * shot], counts[2 * shot + 1]
            cell = cells[shot, item] - base
            entry = (cell << 8) | item
            own[shot, first] = entry
            halo[shot, second] = entry
            mine = ((cell >= begin) & (cell < end)).astype(jnp.int32)
            inside = ((cell >= 0) & (cell < span)).astype(jnp.int32)
            following += [first + mine, second + (inside - mine)]
        return tuple(following)

    counts = lax.fori_loop(0, cells.shape[1], gather, (jnp.int32(0),) * (2 * SHOTS_HERE), unroll=8)
    for shot in range(SHOTS_HERE):
        for number, (entries, count_out) in enumerate(((own, own_count), (halo, halo_count))):
            count = counts[2 * shot + number]
            for extra in range(4):
                entries[shot, count + extra] = -1
            count_out[shot] = count


def unpack_entry(entry):
    plane = (entry >> 20) + (DEEP - SHALLOW)
    depth = PAD + ((entry >> 15) & (NZ - 1))
    lane = ((entry >> 8) & (NY - 1)) | (entry >> 31)
    return plane, depth, lane, entry & (NREC - 1)


def clear_pads(fields):
    zeros = jnp.zeros((ROWS, PAD, NY), jnp.float32)
    for field in fields:
        for shot in range(SHOTS_HERE):
            field[shot, :, 0:PAD, :] = zeros
            field[shot, :, PAD + NZ : DEPTH, :] = zeros


def own_pairs(field, own):
    return [
        (own.at[shot], field.at[shot, pl.ds(DEEP, SLAB), pl.ds(PAD, NZ), :]) for shot in range(SHOTS_HERE)
    ]


def halo_pairs(field, low, high, offset, width):
    pairs = []
    for shot in range(SHOTS_HERE):
        planes = pl.ds(offset + shot * width, width)
        for source, begin in ((low, DEEP - width), (high, DEEP + SLAB)):
            pairs.append((source.at[planes], field.at[shot, pl.ds(begin, width), pl.ds(PAD, NZ), :]))
    return pairs


def place_halo(field, low, high, offset, width):
    for shot in range(SHOTS_HERE):
        begin = offset + shot * width
        field[shot, DEEP - width : DEEP, PAD : PAD + NZ, :] = low[begin : begin + width]
        field[shot, DEEP + SLAB : DEEP + SLAB + width, PAD : PAD + NZ, :] = high[begin : begin + width]


def square_rows(source, start, target, begin, count):
    for row in range(0, count, 4):
        value = source[start + row : start + row + 4]
        target[begin + row : begin + row + 4] = COURANT * value * value


def along_lanes(field, lanes, along, margin):
    first, count = DEEP - margin, SLAB + 2 * margin
    part = count // HALVES
    for shot in range(SHOTS_HERE):
        for half in range(HALVES):
            begin = first + half * part
            block = field[shot, begin : begin + part, PAD : PAD + NZ, :].reshape(part * NZ, NY)
            both = dot(jnp.concatenate(split(block), axis=1), lanes[...])
            along[shot, begin : begin + part] = (both[:, :NY] + both[:, NY:]).reshape(part, NZ, NY)


def leap(field, before, after, speed, along, margin, laplacians=None, slot=None):
    first = DEEP - margin

    @pl.loop(0, (SLAB + 2 * margin) // CHUNK)
    def _(chunk):
        for plane in range(CHUNK):
            here = first + chunk * CHUNK + plane
            for shot in range(SHOTS_HERE):
                spread = along[shot, here]
                for distance in range(1, 5):
                    beside = (
                        field[shot, here + distance, PAD : PAD + NZ, :]
                        + field[shot, here - distance, PAD : PAD + NZ, :]
                    ) + (
                        field[shot, here, PAD + distance : PAD + NZ + distance, :]
                        + field[shot, here, PAD - distance : PAD + NZ - distance, :]
                    )
                    spread = spread + COEFFS[distance] * beside
                centre = field[shot, here, PAD : PAD + NZ, :]
                after[shot, here, PAD : PAD + NZ, :] = (
                    2.0 * centre - before[shot, here, PAD : PAD + NZ, :] + speed[here] * spread
                )
                if laplacians is not None:
                    laplacians[slot, shot, here] = spread


def lane_ids():
    return lax.broadcasted_iota(jnp.int32, (1, NY), 1)


def forward_kernel(
    entries, counts, src, src_counts, signs, wave,
    now, prev, vel, low, high, lanes, noise,
    lap_out, outgoing, speed_out,
    *scratch,
):
    fields = scratch[: STEPS + 2]
    laps, speed, along, samples, sems, out_sems = scratch[STEPS + 2 :]
    copies = started(
        [
            *own_pairs(fields[1], now),
            (vel, speed.at[pl.ds(DEEP, SLAB)]),
            *own_pairs(fields[0], prev),
        ],
        sems,
    )
    place_halo(fields[1], low, high, 0, DEEP)
    place_halo(fields[0], low, high, SHOTS_HERE * DEEP, SHALLOW)
    begin = SHOTS_HERE * (DEEP + SHALLOW)
    square_rows(low, begin, speed, DEEP - SHALLOW, SHALLOW)
    square_rows(high, begin, speed, DEEP + SLAB, SHALLOW)
    clear_pads(fields[1 : STEPS + 1])
    for copy in copies[:2]:
        copy.wait()
    ids = lane_ids()
    outs = []
    for moment in range(STEPS):
        margin = 4 * (STEPS - 1 - moment)
        along_lanes(fields[moment + 1], lanes, along, margin)
        if moment == 0:
            for copy in copies[2:]:
                copy.wait()
            square_rows(speed, DEEP, speed, DEEP, SLAB)
            outs.append(pltpu.make_async_copy(speed, speed_out, out_sems.at[STEPS]))
            outs[0].start()
        leap(fields[moment + 1], fields[moment], fields[moment + 2], speed, along, margin, laps, moment)
        out = pltpu.make_async_copy(laps.at[moment, :, pl.ds(DEEP, SLAB)], lap_out.at[moment], out_sems.at[moment])
        out.start()
        outs.append(out)
        for shot in range(SHOTS_HERE):

            @pl.loop(0, src_counts[shot])
            def _(item, shot=shot):
                plane, depth, lane, which = unpack_entry(src[shot, item])
                amplitude = (2 * signs[shot, which] - 1).astype(jnp.float32) * wave[shot, moment]
                view = fields[moment + 2].at[shot, plane, pl.ds(depth, 1), :]
                view[...] = view[...] + jnp.where(ids == lane, amplitude, 0.0)

    for shot in range(SHOTS_HERE):

        def sample(group, state, shot=shot):
            state = list(state)
            for member in range(4):
                plane, depth, lane, which = unpack_entry(entries[shot, group * 4 + member])
                shift = (which - lane) & (NY - 1)
                hits = [ids == jnp.where(lane >= 0, which - half * NY, -1) for half in range(2)]
                for moment in range(STEPS):
                    line = fields[moment + 2][shot, plane, pl.ds(depth, 1), :]
                    line = pltpu.roll(line, shift, 1)
                    for half in range(2):
                        at = moment * 2 + half
                        state[at] = jnp.where(hits[half], line, state[at])
            return tuple(state)

        zero = jnp.zeros((1, NY), jnp.float32)
        state = lax.fori_loop(0, (counts[shot] + 3) >> 2, sample, (zero,) * (2 * STEPS))
        for moment in range(STEPS):
            for half in range(2):
                line = half * 8 + shot * STEPS + moment
                samples[line : line + 1, :] = state[moment * 2 + half]
    block = samples[...]
    for target in range(16):
        outgoing[target * 24 : target * 24 + 8, :] = noise[target * 8 : target * 8 + 8, :]
        outgoing[target * 24 + 8 : target * 24 + 24, :] = block
    for out in outs:
        out.wait()


def halo_rows(field):
    pairs = []
    for shot in range(SHOTS_HERE):
        for begin in (DEEP - 8, DEEP + SLAB):
            pairs.append(field.at[shot, pl.ds(begin, 8), pl.ds(PAD, NZ), :])
    return pairs


def adjoint_start_kernel(
    now, after, speed_in, low, high, lanes, earlier_out, halo_out, field, later, earlier, speed, along, sems
):
    copies = started(
        [
            *own_pairs(field, now),
            *halo_pairs(field, low, high, 0, DEEP),
            *own_pairs(later, after),
            *halo_pairs(later, low, high, SHOTS_HERE * DEEP, SHALLOW),
            (speed_in, speed),
        ],
        sems,
    )
    clear_pads([field])
    for copy in copies[:6]:
        copy.wait()
    margin = 4 * (STEPS - 1)
    along_lanes(field, lanes, along, margin)
    for copy in copies[6:]:
        copy.wait()
    outs = started([(rows, halo_out.at[place]) for place, rows in enumerate(halo_rows(field))], sems)
    leap(field, later, earlier, speed, along, margin)
    out = pltpu.make_async_copy(earlier.at[:, :, pl.ds(PAD, NZ), :], earlier_out, sems.at[4])
    out.start()
    for copy in outs:
        copy.wait()
    out.wait()


def adjoint_kernel(
    own, own_count, beyond, beyond_count,
    earlier, now, halo, speed_in, vel, laps_in, lanes, incoming, observed,
    tiles,
    *scratch,
):
    fields = [None, *scratch[: STEPS + 1]]
    laps, speed, along, plain, differences, misfit, sems = scratch[STEPS + 1 :]
    copies = started(
        [
            (earlier, fields[2].at[:, :, pl.ds(PAD, NZ), :]),
            *own_pairs(fields[1], now),
            *[(halo.at[place], rows) for place, rows in enumerate(halo_rows(fields[1]))],
            (speed_in, speed),
            (laps_in, laps),
            (vel, plain),
        ],
        sems,
    )
    total = incoming[8:24, :]
    for block in range(1, 16):
        total = total + incoming[block * 24 + 8 : block * 24 + 24, :]
    for shot in range(SHOTS_HERE):
        rows = slice(shot * STEPS, (shot + 1) * STEPS)
        for half in range(2):
            columns = slice(half * NY, (half + 1) * NY)
            differences[rows, columns] = (
                total[half * 8 + shot * STEPS : half * 8 + (shot + 1) * STEPS] - observed[shot, :, columns]
            )
    to_scalars = pltpu.make_async_copy(differences, misfit, sems.at[10])
    to_scalars.start()
    clear_pads(fields[2 : STEPS + 1])
    ids = lane_ids()
    for step in range(STEPS):
        moment = STEPS - step
        if step == 0:
            copies[0].wait()
            to_scalars.wait()
        else:
            margin = 4 * (STEPS - 1 - step)
            along_lanes(fields[step + 1], lanes, along, margin)
            if step == 1:
                for copy in copies[1:8]:
                    copy.wait()
            leap(fields[step + 1], fields[step], fields[step + 2], speed, along, margin)
        for entries, counts in ((own, own_count), (beyond, beyond_count))[: 2 if step < STEPS - 1 else 1]:
            for shot in range(SHOTS_HERE):

                @pl.loop(0, (counts[shot] + 3) >> 2)
                def _(group, entries=entries, shot=shot):
                    for member in range(4):
                        plane, depth, lane, which = unpack_entry(entries[shot, group * 4 + member])
                        value = misfit[shot * STEPS + moment - 1, which]
                        view = fields[step + 2].at[shot, plane, pl.ds(depth, 1), :]
                        view[...] = view[...] + jnp.where(ids == lane, value, 0.0)

    for copy in copies[8:]:
        copy.wait()
    for group in range(SLAB // 4):
        planes = []
        for plane in range(group * 4, group * 4 + 4):
            total = jnp.zeros((NZ, NY), jnp.float32)
            for shot in range(SHOTS_HERE):
                for step in range(STEPS):
                    total = total + (
                        fields[step + 2][shot, DEEP + plane, PAD : PAD + NZ, :]
                        * laps[STEPS - 1 - step, shot, plane]
                    )
            planes.append((2.0 * COURANT) * plain[plane] * total)
        tiles[pl.ds(group, NY, stride=SLAB // 4), :] = jnp.concatenate(planes, axis=0).T


def column_slices(source, target, turned):
    begin = pl.multiple_of(lax.axis_index("shot") * 16, 16)
    for group in range(SLAB // 4):
        turned[...] = source[group * NY : (group + 1) * NY, :].T
        target[pl.ds(group, 16, stride=SLAB // 4), :] = turned[pl.ds(begin, 16), :]


def apply_prior(columns, operators):
    lane = lax.broadcasted_iota(jnp.int32, (NY, NY), 1)
    blocks = []
    for place in range(4):
        turned = columns if place == 0 else pltpu.roll(columns, NY - 32 * place, 1)
        high = turned.astype(jnp.bfloat16).astype(jnp.float32)
        low = pltpu.roll(turned - high, 32, 1)
        blocks.append(jnp.where(lane < 32, high, low).astype(jnp.bfloat16))
    right = jnp.concatenate(blocks, axis=0)
    upper = dot(operators[0], right)
    lower = dot(operators[1], right)
    result = jnp.zeros((NY, NY), jnp.float32)
    for place in range(4):
        rows = slice(place * NY, (place + 1) * NY)
        value = (upper[rows] + lower[rows]) + pltpu.roll(upper[rows], NY - 32, 1)
        value = pltpu.roll(value, 32 * place, 1) if place else value
        result = jnp.where(lane // 32 == place, value, result)
    return result


def noise_kernel(step_size, incoming, operators, velocity, out, velocity_out, turned):
    column_slices(velocity, velocity_out, turned)
    columns = jnp.concatenate([incoming[block * 24 : block * 24 + 8, :] for block in range(16)], axis=0)
    scale = jnp.sqrt(jnp.full((8, NY), step_size[0], jnp.float32))[0:1]
    out[...] = scale * apply_prior(columns, operators)


def prior_kernel(step_size, received, noise, operators, out):
    total = received[0:NY, :]
    for part in range(1, 8):
        total = total + received[part * NY : (part + 1) * NY, :]
    out[...] = (-0.5 * step_size[0]) * apply_prior(total, operators) + noise[...]


def finish_kernel(returned, velocity, out):
    for group in range(SLAB // 4):
        rows = pl.ds(group, 16, stride=SLAB // 4)
        value = returned[rows, :] + velocity[rows, :]
        for place in range(4):
            turned = value if place == 0 else pltpu.roll(value, NY - 32 * place, 1)
            out[group * 4 + place] = turned[:, :NZ]


def shape(*dims, dtype=jnp.float32):
    return jax.ShapeDtypeStruct(dims, dtype)


def pin(values):
    return pltpu.with_memory_space_constraint(values, pltpu.VMEM)


def leave(*values):
    return [pltpu.with_memory_space_constraint(value, pltpu.HBM) for value in values]


def params():
    return pltpu.CompilerParams(vmem_limit_bytes=VMEM_LIMIT)


def neighbours(axis):
    count = lax.axis_size(axis)
    up = [(i, i + 1) for i in range(count - 1)]
    return up, [(b, a) for a, b in up]


def exchange(axis, to_high, to_low):
    up, down = neighbours(axis)
    return lax.ppermute(to_high, axis, up), lax.ppermute(to_low, axis, down)


def body(
    velocity,
    noise_field,
    step_size,
    field_prev,
    field_now,
    adjoint_next,
    adjoint_now,
    wavelet,
    source_cells,
    source_signs,
    record_cells,
    observed,
):
    lanes = jnp.asarray(lane_operator())
    squared, single = (jnp.asarray(operator) for operator in prior_operators())
    planes = SHOTS_HERE * (DEEP + SHALLOW)
    up, down = pl.pallas_call(
        edge_kernel,
        out_shape=(shape(planes + SHALLOW, NZ, NY),) * 2,
        in_specs=[ANY] * 3,
        out_specs=(ANY,) * 2,
        scratch_shapes=[
            *[pltpu.VMEM((planes + SHALLOW, NZ, NY), jnp.float32)] * 2,
            pltpu.SemaphoreType.DMA((2, 10)),
        ],
        name="edges",
    )(field_now, field_prev, velocity)
    low, high = exchange("dom", up, down)
    adjoint_edge, up, down = lax.optimization_barrier((adjoint_now, up, down))

    adj_up, adj_down, noise_tiles, *lists = pl.pallas_call(
        prepare_kernel,
        out_shape=(
            *(shape(planes, NZ, NY),) * 2,
            shape(NY, NY),
            *(shape(SHOTS_HERE, LIST, dtype=jnp.int32), shape(SHOTS_HERE, dtype=jnp.int32)) * 2,
            shape(SHOTS_HERE, 16, dtype=jnp.int32),
            shape(SHOTS_HERE, dtype=jnp.int32),
        ),
        in_specs=[SMEM] * 2 + [ANY] * 2 + [VMEM],
        out_specs=(ANY,) * 2 + (VMEM,) + (SMEM,) * 6,
        scratch_shapes=[
            pltpu.VMEM((NY, NY), jnp.float32),
            *[pltpu.VMEM((planes, NZ, NY), jnp.float32)] * 2,
            pltpu.SemaphoreType.DMA((2, 8)),
        ],
        name="prepare",
    )(
        record_cells, source_cells, adjoint_edge, adjoint_next,
        noise_field.reshape(SLAB * NZ, NY),
    )
    adj_low, adj_high = exchange("dom", adj_up, adj_down)

    fields = [pltpu.VMEM((SHOTS_HERE, ROWS, DEPTH, NY), jnp.float32)] * (STEPS + 2)
    speed = pltpu.VMEM((ROWS, NZ, NY), jnp.float32)
    along = pltpu.VMEM((SHOTS_HERE, ROWS, NZ, NY), jnp.float32)
    laplacians, outgoing, speed_sq = pl.pallas_call(
        forward_kernel,
        out_shape=(
            shape(STEPS, SHOTS_HERE, SLAB, NZ, NY), shape(16 * 24, NY), shape(ROWS, NZ, NY),
        ),
        in_specs=[SMEM] * 6 + [ANY] * 3 + [VMEM] * 4,
        out_specs=(ANY, VMEM, ANY),
        scratch_shapes=[
            *fields,
            pltpu.VMEM((STEPS, SHOTS_HERE, ROWS, NZ, NY), jnp.float32),
            speed,
            along,
            pltpu.VMEM((16, NY), jnp.float32),
            pltpu.SemaphoreType.DMA((5,)),
            pltpu.SemaphoreType.DMA((STEPS + 1,)),
        ],
        compiler_params=params(),
        name="forward_steps",
    )(
        *leave(*lists[:2], *lists[4:], source_signs, wavelet, field_now, field_prev, velocity),
        pin(low), pin(high), *leave(lanes, noise_tiles),
    )

    incoming = lax.all_to_all(outgoing.reshape(16, 24, NY), "dom", 0, 0, tiled=True).reshape(16 * 24, NY)

    field = fields[0]
    earlier, halo = pl.pallas_call(
        adjoint_start_kernel,
        out_shape=(shape(SHOTS_HERE, ROWS, NZ, NY), shape(SHOTS_HERE * 2, 8, NZ, NY)),
        in_specs=[ANY] * 5 + [VMEM],
        out_specs=(ANY,) * 2,
        scratch_shapes=[field, field, field, speed, along, pltpu.SemaphoreType.DMA((13,))],
        compiler_params=params(),
        name="adjoint_start",
    )(*leave(adjoint_now, adjoint_next, speed_sq), pin(adj_low), pin(adj_high), *leave(lanes))
    tiles = pl.pallas_call(
        adjoint_kernel,
        out_shape=shape(SLAB * NZ, NY),
        in_specs=[SMEM] * 4 + [ANY] * 6 + [VMEM] * 3,
        out_specs=VMEM,
        scratch_shapes=[
            *[field] * (STEPS + 1),
            pltpu.VMEM((STEPS, SHOTS_HERE, SLAB, NZ, NY), jnp.float32),
            speed,
            along,
            pltpu.VMEM((SLAB, NZ, NY), jnp.float32),
            pltpu.VMEM((SHOTS_HERE * STEPS, NREC), jnp.float32),
            pltpu.SMEM((SHOTS_HERE * STEPS, NREC), jnp.float32),
            pltpu.SemaphoreType.DMA((11,)),
        ],
        compiler_params=params(),
        name="adjoint_steps",
    )(
        *leave(*lists[:4], earlier, adjoint_now, halo, speed_sq, velocity, laplacians, lanes),
        pin(incoming), *leave(observed),
    )

    noise_update, velocity_tiles = pl.pallas_call(
        noise_kernel,
        out_shape=(shape(NY, NY),) * 2,
        in_specs=[SMEM] + [VMEM] * 3,
        out_specs=(VMEM,) * 2,
        scratch_shapes=[pltpu.VMEM((NY, NY), jnp.float32)],
        name="noise_prior",
    )(step_size, pin(incoming), single, velocity.reshape(SLAB * NZ, NY))

    received = lax.all_to_all(tiles.reshape(128, 8, NY), ("shot", "dom"), 0, 0, tiled=True)
    update = pl.pallas_call(
        prior_kernel,
        out_shape=shape(NY, NY),
        in_specs=[SMEM, VMEM, VMEM, VMEM],
        out_specs=VMEM,
        name="prior",
    )(step_size, pin(received.reshape(128 * 8, NY)), *leave(noise_update), pin(squared))
    returned = lax.all_to_all(update.reshape(16, 8, NY), "dom", 0, 0, tiled=True)
    out = pl.pallas_call(
        finish_kernel,
        out_shape=shape(SLAB, 16, NZ),
        in_specs=[VMEM, VMEM],
        out_specs=VMEM,
        name="finish",
    )(returned.reshape(NY, NY), velocity_tiles)
    return out.transpose(0, 2, 1)


def solution(mesh):
    placed = (
        P("dom", None, None),
        P("dom", None, None),
        P(),
        P("shot", "dom", None, None),
        P("shot", "dom", None, None),
        P("shot", "dom", None, None),
        P("shot", "dom", None, None),
        P("shot", None),
        P("shot", None),
        P("shot", None),
        P("shot", None),
        P("shot", None, None),
    )
    return jax.shard_map(
        body, mesh=mesh, in_specs=placed, out_specs=P("dom", None, "shot"), check_vma=False
    )
```

```python
import math

import jax
import jax.numpy as jnp
import ml_dtypes
import numpy as np
from jax import lax
from jax.experimental import pallas as pl
from jax.experimental.pallas import tpu as pltpu
from jax.sharding import PartitionSpec as P

STEPS = 4
COEFFS = (-205.0 / 72.0, 8.0 / 5.0, -1.0 / 5.0, 8.0 / 315.0, -1.0 / 560.0)
COURANT = 0.02
CUTOFF = 16

NX, NZ, NY = 512, 32, 128
SLAB = 32
DEEP = 16
SHALLOW = 12
ROWS = SLAB + 2 * DEEP
PAD = 8
DEPTH = NZ + 2 * PAD
SHOTS_HERE = 2
NREC = 256
LIST = NREC + 8
CHUNK = 8
HALVES = 1
VMEM_LIMIT = 56 * 1024 * 1024

ANY = pl.BlockSpec(memory_space=pl.ANY)
VMEM = pl.BlockSpec(memory_space=pltpu.VMEM)
SMEM = pl.BlockSpec(memory_space=pltpu.SMEM)


def split_host(matrix):
    high = matrix.astype(ml_dtypes.bfloat16)
    low = (matrix - high.astype(np.float64)).astype(ml_dtypes.bfloat16)
    return high, low


def lane_operator():
    band = np.zeros((NY, NY))
    np.fill_diagonal(band, 3.0 * COEFFS[0])
    for distance in range(1, 5):
        band += COEFFS[distance] * (np.eye(NY, k=distance) + np.eye(NY, k=-distance))
    high, low = split_host(band)
    zero = np.zeros_like(low)
    return np.block([[high, low], [high, zero]])


def prior_operators():
    wave = np.arange(NX)[:, None]
    position = np.arange(NX)[None, :]
    factor = np.where(wave == 0, math.sqrt(1.0 / NX), math.sqrt(2.0 / NX))
    basis = factor * np.cos(math.pi / (2.0 * NX) * (wave * (2 * position + 1) % (4 * NX)))
    gain = 1.0 / np.sqrt(1.0 + np.arange(NX) / CUTOFF)
    order = np.arange(NX).reshape(NX // 4, 4).T.reshape(-1)
    both = []
    for weight in (gain**2, gain):
        operator = basis.T @ (weight[:, None] * basis)
        both.append(np.stack(split_host(operator[order][:, order])))
    return both


def split(values):
    high = values.astype(jnp.bfloat16)
    low = (values - high.astype(jnp.float32)).astype(jnp.bfloat16)
    return high, low


def dot(left, right):
    return jnp.dot(left, right, preferred_element_type=jnp.float32)


def edge_pairs(deep, shallow, velocity, up, down):
    pairs = []
    for target, deep_at, shallow_at in ((up, SLAB - DEEP, SLAB - SHALLOW), (down, 0, 0)):
        for shot in range(SHOTS_HERE):
            pairs.append((deep.at[shot, pl.ds(deep_at, DEEP)], target.at[pl.ds(shot * DEEP, DEEP)]))
            begin = SHOTS_HERE * DEEP + shot * SHALLOW
            pairs.append((shallow.at[shot, pl.ds(shallow_at, SHALLOW)], target.at[pl.ds(begin, SHALLOW)]))
        if velocity is not None:
            begin = SHOTS_HERE * (DEEP + SHALLOW)
            pairs.append((velocity.at[pl.ds(shallow_at, SHALLOW)], target.at[pl.ds(begin, SHALLOW)]))
    return pairs


def started(pairs, sems):
    copies = [pltpu.make_async_copy(source, target, sems.at[n]) for n, (source, target) in enumerate(pairs)]
    for copy in copies:
        copy.start()
    return copies


def stage_edges(deep, shallow, velocity, up, down, staged, sems):
    inward = started(edge_pairs(deep, shallow, velocity, *staged), sems.at[0])
    targets = edge_pairs(deep, shallow, velocity, up, down)
    sources = edge_pairs(deep, shallow, velocity, *staged)
    outward = []
    for number, copy in enumerate(inward):
        copy.wait()
        out = pltpu.make_async_copy(sources[number][1], targets[number][1], sems.at[1, number])
        out.start()
        outward.append(out)
    return outward


def edge_kernel(deep, shallow, velocity, up, down, high, low, sems):
    for copy in stage_edges(deep, shallow, velocity, up, down, (high, low), sems):
        copy.wait()


def prepare_kernel(
    rec, src, deep, shallow, noise,
    up, down, noise_out, own, own_count, halo, halo_count, src_entries, src_counts,
    turned, high, low, sems,
):
    copies = stage_edges(deep, shallow, None, up, down, (high, low), sems)
    list_receivers(rec, own, own_count, halo, halo_count)
    list_cells(src, src_entries, src_counts)
    column_slices(noise, noise_out, turned)
    for copy in copies:
        copy.wait()


def list_cells(cells, entries, count_out):
    base = (lax.axis_index("dom") * SLAB - SHALLOW) * (NZ * NY)
    span = (SLAB + 2 * SHALLOW) * NZ * NY

    def gather(item, counts):
        following = []
        for shot in range(SHOTS_HERE):
            cell = cells[shot, item] - base
            entries[shot, counts[shot]] = (cell << 8) | item
            inside = (cell >= 0) & (cell < span)
            following.append(counts[shot] + inside.astype(jnp.int32))
        return tuple(following)

    counts = lax.fori_loop(0, cells.shape[1], gather, (jnp.int32(0),) * SHOTS_HERE, unroll=8)
    for shot in range(SHOTS_HERE):
        for extra in range(4):
            entries[shot, counts[shot] + extra] = -1
        count_out[shot] = counts[shot]


def list_receivers(cells, own, own_count, halo, halo_count):
    base = (lax.axis_index("dom") * SLAB - SHALLOW) * (NZ * NY)
    begin, end = SHALLOW * NZ * NY, (SHALLOW + SLAB) * NZ * NY
    span = (SLAB + 2 * SHALLOW) * NZ * NY

    def gather(item, counts):
        following = []
        for shot in range(SHOTS_HERE):
            first, second = counts[2 * shot], counts[2 * shot + 1]
            cell = cells[shot, item] - base
            entry = (cell << 8) | item
            own[shot, first] = entry
            halo[shot, second] = entry
            mine = ((cell >= begin) & (cell < end)).astype(jnp.int32)
            inside = ((cell >= 0) & (cell < span)).astype(jnp.int32)
            following += [first + mine, second + (inside - mine)]
        return tuple(following)

    counts = lax.fori_loop(0, cells.shape[1], gather, (jnp.int32(0),) * (2 * SHOTS_HERE), unroll=8)
    for shot in range(SHOTS_HERE):
        for number, (entries, count_out) in enumerate(((own, own_count), (halo, halo_count))):
            count = counts[2 * shot + number]
            for extra in range(4):
                entries[shot, count + extra] = -1
            count_out[shot] = count


def unpack_entry(entry):
    plane = (entry >> 20) + (DEEP - SHALLOW)
    depth = PAD + ((entry >> 15) & (NZ - 1))
    lane = ((entry >> 8) & (NY - 1)) | (entry >> 31)
    return plane, depth, lane, entry & (NREC - 1)


def clear_pads(fields):
    zeros = jnp.zeros((ROWS, PAD, NY), jnp.float32)
    for field in fields:
        for shot in range(SHOTS_HERE):
            field[shot, :, 0:PAD, :] = zeros
            field[shot, :, PAD + NZ : DEPTH, :] = zeros


def own_pairs(field, own):
    return [
        (own.at[shot], field.at[shot, pl.ds(DEEP, SLAB), pl.ds(PAD, NZ), :]) for shot in range(SHOTS_HERE)
    ]


def halo_pairs(field, low, high, offset, width):
    pairs = []
    for shot in range(SHOTS_HERE):
        planes = pl.ds(offset + shot * width, width)
        for source, begin in ((low, DEEP - width), (high, DEEP + SLAB)):
            pairs.append((source.at[planes], field.at[shot, pl.ds(begin, width), pl.ds(PAD, NZ), :]))
    return pairs


def place_halo(field, low, high, offset, width):
    for shot in range(SHOTS_HERE):
        begin = offset + shot * width
        field[shot, DEEP - width : DEEP, PAD : PAD + NZ, :] = low[begin : begin + width]
        field[shot, DEEP + SLAB : DEEP + SLAB + width, PAD : PAD + NZ, :] = high[begin : begin + width]


def square_rows(source, start, target, begin, count):
    for row in range(0, count, 4):
        value = source[start + row : start + row + 4]
        target[begin + row : begin + row + 4] = COURANT * value * value


def along_lanes(field, lanes, along, margin):
    first, count = DEEP - margin, SLAB + 2 * margin
    part = count // HALVES
    for shot in range(SHOTS_HERE):
        for half in range(HALVES):
            begin = first + half * part
            block = field[shot, begin : begin + part, PAD : PAD + NZ, :].reshape(part * NZ, NY)
            both = dot(jnp.concatenate(split(block), axis=1), lanes[...])
            along[shot, begin : begin + part] = (both[:, :NY] + both[:, NY:]).reshape(part, NZ, NY)


def leap(field, before, after, speed, along, margin, laplacians=None, slot=None, chunks=None):
    first = DEEP - margin

    @pl.loop(*(chunks or (0, (SLAB + 2 * margin) // CHUNK)))
    def _(chunk):
        for plane in range(CHUNK):
            here = first + chunk * CHUNK + plane
            for shot in range(SHOTS_HERE):
                spread = along[shot, here]
                for distance in range(1, 5):
                    beside = (
                        field[shot, here + distance, PAD : PAD + NZ, :]
                        + field[shot, here - distance, PAD : PAD + NZ, :]
                    ) + (
                        field[shot, here, PAD + distance : PAD + NZ + distance, :]
                        + field[shot, here, PAD - distance : PAD + NZ - distance, :]
                    )
                    spread = spread + COEFFS[distance] * beside
                centre = field[shot, here, PAD : PAD + NZ, :]
                after[shot, here, PAD : PAD + NZ, :] = (
                    2.0 * centre - before[shot, here, PAD : PAD + NZ, :] + speed[here] * spread
                )
                if laplacians is not None:
                    laplacians[slot, shot, here] = spread


def lane_ids():
    return lax.broadcasted_iota(jnp.int32, (1, NY), 1)


def forward_kernel(
    entries, counts, src, src_counts, signs, wave,
    now, prev, vel, low, high, lanes, noise,
    lap_out, outgoing, speed_out,
    *scratch,
):
    fields = scratch[: STEPS + 2]
    laps, speed, along, samples, sems, out_sems = scratch[STEPS + 2 :]
    copies = started(
        [
            *own_pairs(fields[1], now),
            (vel, speed.at[pl.ds(DEEP, SLAB)]),
            *own_pairs(fields[0], prev),
        ],
        sems,
    )
    place_halo(fields[1], low, high, 0, DEEP)
    place_halo(fields[0], low, high, SHOTS_HERE * DEEP, SHALLOW)
    begin = SHOTS_HERE * (DEEP + SHALLOW)
    square_rows(low, begin, speed, DEEP - SHALLOW, SHALLOW)
    square_rows(high, begin, speed, DEEP + SLAB, SHALLOW)
    clear_pads(fields[1 : STEPS + 1])
    for copy in copies[:2]:
        copy.wait()
    ids = lane_ids()
    outs = []
    for moment in range(STEPS):
        margin = 4 * (STEPS - 1 - moment)
        along_lanes(fields[moment + 1], lanes, along, margin)
        if moment == 0:
            for copy in copies[2:]:
                copy.wait()
            square_rows(speed, DEEP, speed, DEEP, SLAB)
            outs.append(pltpu.make_async_copy(speed, speed_out, out_sems.at[STEPS]))
            outs[0].start()
        leap(fields[moment + 1], fields[moment], fields[moment + 2], speed, along, margin, laps, moment)
        out = pltpu.make_async_copy(laps.at[moment, :, pl.ds(DEEP, SLAB)], lap_out.at[moment], out_sems.at[moment])
        out.start()
        outs.append(out)
        for shot in range(SHOTS_HERE):

            @pl.loop(0, src_counts[shot])
            def _(item, shot=shot):
                plane, depth, lane, which = unpack_entry(src[shot, item])
                amplitude = (2 * signs[shot, which] - 1).astype(jnp.float32) * wave[shot, moment]
                view = fields[moment + 2].at[shot, plane, pl.ds(depth, 1), :]
                view[...] = view[...] + jnp.where(ids == lane, amplitude, 0.0)

    for shot in range(SHOTS_HERE):

        def sample(group, state, shot=shot):
            state = list(state)
            for member in range(4):
                plane, depth, lane, which = unpack_entry(entries[shot, group * 4 + member])
                shift = (which - lane) & (NY - 1)
                hits = [ids == jnp.where(lane >= 0, which - half * NY, -1) for half in range(2)]
                for moment in range(STEPS):
                    line = fields[moment + 2][shot, plane, pl.ds(depth, 1), :]
                    line = pltpu.roll(line, shift, 1)
                    for half in range(2):
                        at = moment * 2 + half
                        state[at] = jnp.where(hits[half], line, state[at])
            return tuple(state)

        zero = jnp.zeros((1, NY), jnp.float32)
        state = lax.fori_loop(0, (counts[shot] + 3) >> 2, sample, (zero,) * (2 * STEPS))
        for moment in range(STEPS):
            for half in range(2):
                line = half * 8 + shot * STEPS + moment
                samples[line : line + 1, :] = state[moment * 2 + half]
    block = samples[...]
    for target in range(16):
        outgoing[target * 24 : target * 24 + 8, :] = noise[target * 8 : target * 8 + 8, :]
        outgoing[target * 24 + 8 : target * 24 + 24, :] = block
    for out in outs:
        out.wait()


def halo_rows(field):
    pairs = []
    for shot in range(SHOTS_HERE):
        for begin in (DEEP - 8, DEEP + SLAB):
            pairs.append(field.at[shot, pl.ds(begin, 8), pl.ds(PAD, NZ), :])
    return pairs


def adjoint_start_kernel(
    now, after, speed_in, low, high, lanes, earlier_out, halo_out, field, later, earlier, speed, along, sems
):
    copies = started(
        [
            *own_pairs(field, now),
            *halo_pairs(field, low, high, 0, DEEP),
            *own_pairs(later, after),
            *halo_pairs(later, low, high, SHOTS_HERE * DEEP, SHALLOW),
            (speed_in, speed),
        ],
        sems,
    )
    clear_pads([field])
    for copy in copies[:6]:
        copy.wait()
    margin = 4 * (STEPS - 1)
    along_lanes(field, lanes, along, margin)
    for copy in copies[6:]:
        copy.wait()
    outs = started([(rows, halo_out.at[place]) for place, rows in enumerate(halo_rows(field))], sems)
    for number, chunks in enumerate(((0, 3), (3, 5), (5, 7))):
        leap(field, later, earlier, speed, along, margin, chunks=chunks)
        rows = pl.ds(DEEP - margin + chunks[0] * CHUNK, (chunks[1] - chunks[0]) * CHUNK)
        source = earlier.at[:, rows, pl.ds(PAD, NZ), :]
        out = pltpu.make_async_copy(source, earlier_out.at[:, rows], sems.at[4 + number])
        out.start()
        outs.append(out)
    for copy in outs:
        copy.wait()


def adjoint_kernel(
    own, own_count, beyond, beyond_count,
    earlier, now, halo, speed_in, vel, laps_in, lanes, incoming, observed,
    tiles,
    *scratch,
):
    fields = [None, *scratch[: STEPS + 1]]
    laps, speed, along, plain, differences, misfit, sems = scratch[STEPS + 1 :]
    copies = started(
        [
            (
                earlier.at[:, pl.ds(DEEP - SHALLOW, SLAB + 2 * SHALLOW)],
                fields[2].at[:, pl.ds(DEEP - SHALLOW, SLAB + 2 * SHALLOW), pl.ds(PAD, NZ), :],
            ),
            *own_pairs(fields[1], now),
            *[(halo.at[place], rows) for place, rows in enumerate(halo_rows(fields[1]))],
            (speed_in, speed),
            (laps_in, laps),
            (vel, plain),
        ],
        sems,
    )
    total = incoming[8:24, :]
    for block in range(1, 16):
        total = total + incoming[block * 24 + 8 : block * 24 + 24, :]
    for shot in range(SHOTS_HERE):
        rows = slice(shot * STEPS, (shot + 1) * STEPS)
        for half in range(2):
            columns = slice(half * NY, (half + 1) * NY)
            differences[rows, columns] = (
                total[half * 8 + shot * STEPS : half * 8 + (shot + 1) * STEPS] - observed[shot, :, columns]
            )
    to_scalars = pltpu.make_async_copy(differences, misfit, sems.at[10])
    to_scalars.start()
    clear_pads(fields[2 : STEPS + 1])
    ids = lane_ids()
    for step in range(STEPS):
        moment = STEPS - step
        if step == 0:
            copies[0].wait()
            to_scalars.wait()
        else:
            margin = 4 * (STEPS - 1 - step)
            along_lanes(fields[step + 1], lanes, along, margin)
            if step == 1:
                for copy in copies[1:8]:
                    copy.wait()
            leap(fields[step + 1], fields[step], fields[step + 2], speed, along, margin)
        for entries, counts in ((own, own_count), (beyond, beyond_count))[: 2 if step < STEPS - 1 else 1]:
            for shot in range(SHOTS_HERE):

                @pl.loop(0, (counts[shot] + 3) >> 2)
                def _(group, entries=entries, shot=shot):
                    for member in range(4):
                        plane, depth, lane, which = unpack_entry(entries[shot, group * 4 + member])
                        value = misfit[shot * STEPS + moment - 1, which]
                        view = fields[step + 2].at[shot, plane, pl.ds(depth, 1), :]
                        view[...] = view[...] + jnp.where(ids == lane, value, 0.0)

    for copy in copies[8:]:
        copy.wait()
    for group in range(SLAB // 4):
        planes = []
        for plane in range(group * 4, group * 4 + 4):
            total = jnp.zeros((NZ, NY), jnp.float32)
            for shot in range(SHOTS_HERE):
                for step in range(STEPS):
                    total = total + (
                        fields[step + 2][shot, DEEP + plane, PAD : PAD + NZ, :]
                        * laps[STEPS - 1 - step, shot, plane]
                    )
            planes.append((2.0 * COURANT) * plain[plane] * total)
        tiles[pl.ds(group, NY, stride=SLAB // 4), :] = jnp.concatenate(planes, axis=0).T


def column_slices(source, target, turned):
    begin = pl.multiple_of(lax.axis_index("shot") * 16, 16)
    for group in range(SLAB // 4):
        turned[...] = source[group * NY : (group + 1) * NY, :].T
        target[pl.ds(group, 16, stride=SLAB // 4), :] = turned[pl.ds(begin, 16), :]


def apply_prior(columns, operators):
    lane = lax.broadcasted_iota(jnp.int32, (NY, NY), 1)
    blocks = []
    for place in range(4):
        turned = columns if place == 0 else pltpu.roll(columns, NY - 32 * place, 1)
        high = turned.astype(jnp.bfloat16).astype(jnp.float32)
        low = pltpu.roll(turned - high, 32, 1)
        blocks.append(jnp.where(lane < 32, high, low).astype(jnp.bfloat16))
    right = jnp.concatenate(blocks, axis=0)
    upper = dot(operators[0], right)
    lower = dot(operators[1], right)
    result = jnp.zeros((NY, NY), jnp.float32)
    for place in range(4):
        rows = slice(place * NY, (place + 1) * NY)
        value = (upper[rows] + lower[rows]) + pltpu.roll(upper[rows], NY - 32, 1)
        value = pltpu.roll(value, 32 * place, 1) if place else value
        result = jnp.where(lane // 32 == place, value, result)
    return result


def noise_kernel(step_size, incoming, operators, velocity, out, velocity_out, turned):
    column_slices(velocity, velocity_out, turned)
    columns = jnp.concatenate([incoming[block * 24 : block * 24 + 8, :] for block in range(16)], axis=0)
    scale = jnp.sqrt(jnp.full((8, NY), step_size[0], jnp.float32))[0:1]
    out[...] = scale * apply_prior(columns, operators)


def prior_kernel(step_size, received, noise, operators, out):
    total = received[0:NY, :]
    for part in range(1, 8):
        total = total + received[part * NY : (part + 1) * NY, :]
    out[...] = (-0.5 * step_size[0]) * apply_prior(total, operators) + noise[...]


def finish_kernel(returned, velocity, out):
    for group in range(SLAB // 4):
        rows = pl.ds(group, 16, stride=SLAB // 4)
        value = returned[rows, :] + velocity[rows, :]
        for place in range(4):
            turned = value if place == 0 else pltpu.roll(value, NY - 32 * place, 1)
            out[group * 4 + place] = turned[:, :NZ]


def shape(*dims, dtype=jnp.float32):
    return jax.ShapeDtypeStruct(dims, dtype)


def pin(values):
    return pltpu.with_memory_space_constraint(values, pltpu.VMEM)


def leave(*values):
    return [pltpu.with_memory_space_constraint(value, pltpu.HBM) for value in values]


def params():
    return pltpu.CompilerParams(vmem_limit_bytes=VMEM_LIMIT)


def neighbours(axis):
    count = lax.axis_size(axis)
    up = [(i, i + 1) for i in range(count - 1)]
    return up, [(b, a) for a, b in up]


def exchange(axis, to_high, to_low):
    up, down = neighbours(axis)
    return lax.ppermute(to_high, axis, up), lax.ppermute(to_low, axis, down)


def body(
    velocity,
    noise_field,
    step_size,
    field_prev,
    field_now,
    adjoint_next,
    adjoint_now,
    wavelet,
    source_cells,
    source_signs,
    record_cells,
    observed,
):
    lanes = jnp.asarray(lane_operator())
    squared, single = (jnp.asarray(operator) for operator in prior_operators())
    planes = SHOTS_HERE * (DEEP + SHALLOW)
    up, down = pl.pallas_call(
        edge_kernel,
        out_shape=(shape(planes + SHALLOW, NZ, NY),) * 2,
        in_specs=[ANY] * 3,
        out_specs=(ANY,) * 2,
        scratch_shapes=[
            *[pltpu.VMEM((planes + SHALLOW, NZ, NY), jnp.float32)] * 2,
            pltpu.SemaphoreType.DMA((2, 10)),
        ],
        name="edges",
    )(field_now, field_prev, velocity)
    low, high = exchange("dom", up, down)
    adjoint_edge, up, down = lax.optimization_barrier((adjoint_now, up, down))

    adj_up, adj_down, noise_tiles, *lists = pl.pallas_call(
        prepare_kernel,
        out_shape=(
            *(shape(planes, NZ, NY),) * 2,
            shape(NY, NY),
            *(shape(SHOTS_HERE, LIST, dtype=jnp.int32), shape(SHOTS_HERE, dtype=jnp.int32)) * 2,
            shape(SHOTS_HERE, 16, dtype=jnp.int32),
            shape(SHOTS_HERE, dtype=jnp.int32),
        ),
        in_specs=[SMEM] * 2 + [ANY] * 2 + [VMEM],
        out_specs=(ANY,) * 2 + (VMEM,) + (SMEM,) * 6,
        scratch_shapes=[
            pltpu.VMEM((NY, NY), jnp.float32),
            *[pltpu.VMEM((planes, NZ, NY), jnp.float32)] * 2,
            pltpu.SemaphoreType.DMA((2, 8)),
        ],
        name="prepare",
    )(
        record_cells, source_cells, adjoint_edge, adjoint_next,
        noise_field.reshape(SLAB * NZ, NY),
    )
    adj_low, adj_high = exchange("dom", adj_up, adj_down)

    fields = [pltpu.VMEM((SHOTS_HERE, ROWS, DEPTH, NY), jnp.float32)] * (STEPS + 2)
    speed = pltpu.VMEM((ROWS, NZ, NY), jnp.float32)
    along = pltpu.VMEM((SHOTS_HERE, ROWS, NZ, NY), jnp.float32)
    laplacians, outgoing, speed_sq = pl.pallas_call(
        forward_kernel,
        out_shape=(
            shape(STEPS, SHOTS_HERE, SLAB, NZ, NY), shape(16 * 24, NY), shape(ROWS, NZ, NY),
        ),
        in_specs=[SMEM] * 6 + [ANY] * 3 + [VMEM] * 4,
        out_specs=(ANY, VMEM, ANY),
        scratch_shapes=[
            *fields,
            pltpu.VMEM((STEPS, SHOTS_HERE, ROWS, NZ, NY), jnp.float32),
            speed,
            along,
            pltpu.VMEM((16, NY), jnp.float32),
            pltpu.SemaphoreType.DMA((5,)),
            pltpu.SemaphoreType.DMA((STEPS + 1,)),
        ],
        compiler_params=params(),
        name="forward_steps",
    )(
        *leave(*lists[:2], *lists[4:], source_signs, wavelet, field_now, field_prev, velocity),
        pin(low), pin(high), *leave(lanes, noise_tiles),
    )

    incoming = lax.all_to_all(outgoing.reshape(16, 24, NY), "dom", 0, 0, tiled=True).reshape(16 * 24, NY)

    field = fields[0]
    earlier, halo = pl.pallas_call(
        adjoint_start_kernel,
        out_shape=(shape(SHOTS_HERE, ROWS, NZ, NY), shape(SHOTS_HERE * 2, 8, NZ, NY)),
        in_specs=[ANY] * 5 + [VMEM],
        out_specs=(ANY,) * 2,
        scratch_shapes=[field, field, field, speed, along, pltpu.SemaphoreType.DMA((13,))],
        compiler_params=params(),
        name="adjoint_start",
    )(*leave(adjoint_now, adjoint_next, speed_sq), pin(adj_low), pin(adj_high), *leave(lanes))
    tiles = pl.pallas_call(
        adjoint_kernel,
        out_shape=shape(SLAB * NZ, NY),
        in_specs=[SMEM] * 4 + [ANY] * 6 + [VMEM] * 3,
        out_specs=VMEM,
        scratch_shapes=[
            *[field] * (STEPS + 1),
            pltpu.VMEM((STEPS, SHOTS_HERE, SLAB, NZ, NY), jnp.float32),
            speed,
            along,
            pltpu.VMEM((SLAB, NZ, NY), jnp.float32),
            pltpu.VMEM((SHOTS_HERE * STEPS, NREC), jnp.float32),
            pltpu.SMEM((SHOTS_HERE * STEPS, NREC), jnp.float32),
            pltpu.SemaphoreType.DMA((11,)),
        ],
        compiler_params=params(),
        name="adjoint_steps",
    )(
        *leave(*lists[:4], earlier, adjoint_now, halo, speed_sq, velocity, laplacians, lanes),
        pin(incoming), *leave(observed),
    )

    noise_update, velocity_tiles = pl.pallas_call(
        noise_kernel,
        out_shape=(shape(NY, NY),) * 2,
        in_specs=[SMEM] + [VMEM] * 3,
        out_specs=(VMEM,) * 2,
        scratch_shapes=[pltpu.VMEM((NY, NY), jnp.float32)],
        name="noise_prior",
    )(step_size, pin(incoming), single, velocity.reshape(SLAB * NZ, NY))

    received = lax.all_to_all(tiles.reshape(128, 8, NY), ("shot", "dom"), 0, 0, tiled=True)
    update = pl.pallas_call(
        prior_kernel,
        out_shape=shape(NY, NY),
        in_specs=[SMEM, VMEM, VMEM, VMEM],
        out_specs=VMEM,
        name="prior",
    )(step_size, pin(received.reshape(128 * 8, NY)), *leave(noise_update), pin(squared))
    returned = lax.all_to_all(update.reshape(16, 8, NY), "dom", 0, 0, tiled=True)
    out = pl.pallas_call(
        finish_kernel,
        out_shape=shape(SLAB, 16, NZ),
        in_specs=[VMEM, VMEM],
        out_specs=VMEM,
        name="finish",
    )(returned.reshape(NY, NY), velocity_tiles)
    return out.transpose(0, 2, 1)


def solution(mesh):
    placed = (
        P("dom", None, None),
        P("dom", None, None),
        P(),
        P("shot", "dom", None, None),
        P("shot", "dom", None, None),
        P("shot", "dom", None, None),
        P("shot", "dom", None, None),
        P("shot", None),
        P("shot", None),
        P("shot", None),
        P("shot", None),
        P("shot", None, None),
    )
    return jax.shard_map(
        body, mesh=mesh, in_specs=placed, out_specs=P("dom", None, "shot"), check_vma=False
    )
```

```python
import math

import jax
import jax.numpy as jnp
import ml_dtypes
import numpy as np
from jax import lax
from jax.experimental import pallas as pl
from jax.experimental.pallas import tpu as pltpu
from jax.sharding import PartitionSpec as P

STEPS = 4
COEFFS = (-205.0 / 72.0, 8.0 / 5.0, -1.0 / 5.0, 8.0 / 315.0, -1.0 / 560.0)
COURANT = 0.02
CUTOFF = 16

NX, NZ, NY = 512, 32, 128
SLAB = 32
DEEP = 16
SHALLOW = 12
ROWS = SLAB + 2 * DEEP
PAD = 8
DEPTH = NZ + 2 * PAD
SHOTS_HERE = 2
NREC = 256
LIST = NREC + 8
CHUNK = 8
HALVES = 1
VMEM_LIMIT = 56 * 1024 * 1024

ANY = pl.BlockSpec(memory_space=pl.ANY)
VMEM = pl.BlockSpec(memory_space=pltpu.VMEM)
SMEM = pl.BlockSpec(memory_space=pltpu.SMEM)


def split_host(matrix):
    high = matrix.astype(ml_dtypes.bfloat16)
    low = (matrix - high.astype(np.float64)).astype(ml_dtypes.bfloat16)
    return high, low


def lane_operator():
    band = np.zeros((NY, NY))
    np.fill_diagonal(band, 3.0 * COEFFS[0])
    for distance in range(1, 5):
        band += COEFFS[distance] * (np.eye(NY, k=distance) + np.eye(NY, k=-distance))
    high, low = split_host(band)
    zero = np.zeros_like(low)
    return np.block([[high, low], [high, zero]])


def prior_operators():
    wave = np.arange(NX)[:, None]
    position = np.arange(NX)[None, :]
    factor = np.where(wave == 0, math.sqrt(1.0 / NX), math.sqrt(2.0 / NX))
    basis = factor * np.cos(math.pi / (2.0 * NX) * (wave * (2 * position + 1) % (4 * NX)))
    gain = 1.0 / np.sqrt(1.0 + np.arange(NX) / CUTOFF)
    order = np.arange(NX).reshape(NX // 4, 4).T.reshape(-1)
    both = []
    for weight in (gain**2, gain):
        operator = basis.T @ (weight[:, None] * basis)
        both.append(np.stack(split_host(operator[order][:, order])))
    return both


def split(values):
    high = values.astype(jnp.bfloat16)
    low = (values - high.astype(jnp.float32)).astype(jnp.bfloat16)
    return high, low


def dot(left, right):
    return jnp.dot(left, right, preferred_element_type=jnp.float32)


def edge_pairs(deep, shallow, velocity, up, down):
    pairs = []
    for target, deep_at, shallow_at in ((up, SLAB - DEEP, SLAB - SHALLOW), (down, 0, 0)):
        for shot in range(SHOTS_HERE):
            pairs.append((deep.at[shot, pl.ds(deep_at, DEEP)], target.at[pl.ds(shot * DEEP, DEEP)]))
            begin = SHOTS_HERE * DEEP + shot * SHALLOW
            pairs.append((shallow.at[shot, pl.ds(shallow_at, SHALLOW)], target.at[pl.ds(begin, SHALLOW)]))
        if velocity is not None:
            begin = SHOTS_HERE * (DEEP + SHALLOW)
            pairs.append((velocity.at[pl.ds(shallow_at, SHALLOW)], target.at[pl.ds(begin, SHALLOW)]))
    return pairs


def started(pairs, sems):
    copies = [pltpu.make_async_copy(source, target, sems.at[n]) for n, (source, target) in enumerate(pairs)]
    for copy in copies:
        copy.start()
    return copies


def stage_edges(deep, shallow, velocity, up, down, staged, sems):
    inward = started(edge_pairs(deep, shallow, velocity, *staged), sems.at[0])
    targets = edge_pairs(deep, shallow, velocity, up, down)
    sources = edge_pairs(deep, shallow, velocity, *staged)
    outward = []
    for number, copy in enumerate(inward):
        copy.wait()
        out = pltpu.make_async_copy(sources[number][1], targets[number][1], sems.at[1, number])
        out.start()
        outward.append(out)
    return outward


def edge_kernel(deep, shallow, velocity, up, down, high, low, sems):
    for copy in stage_edges(deep, shallow, velocity, up, down, (high, low), sems):
        copy.wait()


def prepare_kernel(
    rec, src, deep, shallow, noise,
    up, down, noise_out, own, own_count, halo, halo_count, src_entries, src_counts,
    turned, high, low, sems,
):
    copies = stage_edges(deep, shallow, None, up, down, (high, low), sems)
    list_receivers(rec, own, own_count, halo, halo_count)
    list_cells(src, src_entries, src_counts)
    column_slices(noise, noise_out, turned)
    for copy in copies:
        copy.wait()


def list_cells(cells, entries, count_out):
    base = (lax.axis_index("dom") * SLAB - SHALLOW) * (NZ * NY)
    span = (SLAB + 2 * SHALLOW) * NZ * NY

    def gather(item, counts):
        following = []
        for shot in range(SHOTS_HERE):
            cell = cells[shot, item] - base
            entries[shot, counts[shot]] = (cell << 8) | item
            inside = (cell >= 0) & (cell < span)
            following.append(counts[shot] + inside.astype(jnp.int32))
        return tuple(following)

    counts = lax.fori_loop(0, cells.shape[1], gather, (jnp.int32(0),) * SHOTS_HERE, unroll=8)
    for shot in range(SHOTS_HERE):
        for extra in range(4):
            entries[shot, counts[shot] + extra] = -1
        count_out[shot] = counts[shot]


def list_receivers(cells, own, own_count, halo, halo_count):
    base = (lax.axis_index("dom") * SLAB - SHALLOW) * (NZ * NY)
    begin, end = SHALLOW * NZ * NY, (SHALLOW + SLAB) * NZ * NY
    span = (SLAB + 2 * SHALLOW) * NZ * NY

    def gather(item, counts):
        following = []
        for shot in range(SHOTS_HERE):
            first, second = counts[2 * shot], counts[2 * shot + 1]
            cell = cells[shot, item] - base
            entry = (cell << 8) | item
            own[shot, first] = entry
            halo[shot, second] = entry
            mine = ((cell >= begin) & (cell < end)).astype(jnp.int32)
            inside = ((cell >= 0) & (cell < span)).astype(jnp.int32)
            following += [first + mine, second + (inside - mine)]
        return tuple(following)

    counts = lax.fori_loop(0, cells.shape[1], gather, (jnp.int32(0),) * (2 * SHOTS_HERE), unroll=8)
    for shot in range(SHOTS_HERE):
        for number, (entries, count_out) in enumerate(((own, own_count), (halo, halo_count))):
            count = counts[2 * shot + number]
            for extra in range(4):
                entries[shot, count + extra] = -1
            count_out[shot] = count


def unpack_entry(entry):
    plane = (entry >> 20) + (DEEP - SHALLOW)
    depth = PAD + ((entry >> 15) & (NZ - 1))
    lane = ((entry >> 8) & (NY - 1)) | (entry >> 31)
    return plane, depth, lane, entry & (NREC - 1)


def clear_pads(fields):
    zeros = jnp.zeros((ROWS, PAD, NY), jnp.float32)
    for field in fields:
        for shot in range(SHOTS_HERE):
            field[shot, :, 0:PAD, :] = zeros
            field[shot, :, PAD + NZ : DEPTH, :] = zeros


def own_pairs(field, own):
    return [
        (own.at[shot], field.at[shot, pl.ds(DEEP, SLAB), pl.ds(PAD, NZ), :]) for shot in range(SHOTS_HERE)
    ]


def halo_pairs(field, low, high, offset, width):
    pairs = []
    for shot in range(SHOTS_HERE):
        planes = pl.ds(offset + shot * width, width)
        for source, begin in ((low, DEEP - width), (high, DEEP + SLAB)):
            pairs.append((source.at[planes], field.at[shot, pl.ds(begin, width), pl.ds(PAD, NZ), :]))
    return pairs


def place_halo(field, low, high, offset, width):
    for shot in range(SHOTS_HERE):
        begin = offset + shot * width
        field[shot, DEEP - width : DEEP, PAD : PAD + NZ, :] = low[begin : begin + width]
        field[shot, DEEP + SLAB : DEEP + SLAB + width, PAD : PAD + NZ, :] = high[begin : begin + width]


def square_rows(source, start, target, begin, count):
    for row in range(0, count, 4):
        value = source[start + row : start + row + 4]
        target[begin + row : begin + row + 4] = COURANT * value * value


def along_lanes(field, lanes, along, margin):
    first, count = DEEP - margin, SLAB + 2 * margin
    part = count // HALVES
    for shot in range(SHOTS_HERE):
        for half in range(HALVES):
            begin = first + half * part
            block = field[shot, begin : begin + part, PAD : PAD + NZ, :].reshape(part * NZ, NY)
            both = dot(jnp.concatenate(split(block), axis=1), lanes[...])
            along[shot, begin : begin + part] = (both[:, :NY] + both[:, NY:]).reshape(part, NZ, NY)


def leap(field, before, after, speed, along, margin, laplacians=None, slot=None, chunks=None):
    first = DEEP - margin

    @pl.loop(*(chunks or (0, (SLAB + 2 * margin) // CHUNK)))
    def _(chunk):
        for plane in range(CHUNK):
            here = first + chunk * CHUNK + plane
            for shot in range(SHOTS_HERE):
                spread = along[shot, here]
                for distance in range(1, 5):
                    beside = (
                        field[shot, here + distance, PAD : PAD + NZ, :]
                        + field[shot, here - distance, PAD : PAD + NZ, :]
                    ) + (
                        field[shot, here, PAD + distance : PAD + NZ + distance, :]
                        + field[shot, here, PAD - distance : PAD + NZ - distance, :]
                    )
                    spread = spread + COEFFS[distance] * beside
                centre = field[shot, here, PAD : PAD + NZ, :]
                after[shot, here, PAD : PAD + NZ, :] = (
                    2.0 * centre - before[shot, here, PAD : PAD + NZ, :] + speed[here] * spread
                )
                if laplacians is not None:
                    laplacians[slot, shot, here] = spread


def lane_ids():
    return lax.broadcasted_iota(jnp.int32, (1, NY), 1)


def forward_kernel(
    entries, counts, src, src_counts, signs, wave,
    now, prev, vel, low, high, lanes, noise,
    lap_out, outgoing, speed_out,
    *scratch,
):
    fields = scratch[: STEPS + 2]
    laps, speed, along, samples, sems, out_sems = scratch[STEPS + 2 :]
    copies = started(
        [
            *own_pairs(fields[1], now),
            (vel, speed.at[pl.ds(DEEP, SLAB)]),
            *own_pairs(fields[0], prev),
        ],
        sems,
    )
    place_halo(fields[1], low, high, 0, DEEP)
    place_halo(fields[0], low, high, SHOTS_HERE * DEEP, SHALLOW)
    begin = SHOTS_HERE * (DEEP + SHALLOW)
    square_rows(low, begin, speed, DEEP - SHALLOW, SHALLOW)
    square_rows(high, begin, speed, DEEP + SLAB, SHALLOW)
    clear_pads(fields[1:2])
    for copy in copies[:2]:
        copy.wait()
    ids = lane_ids()
    outs = []
    for moment in range(STEPS):
        margin = 4 * (STEPS - 1 - moment)
        along_lanes(fields[moment + 1], lanes, along, margin)
        if moment == 0:
            clear_pads(fields[2 : STEPS + 1])
            for copy in copies[2:]:
                copy.wait()
            square_rows(speed, DEEP, speed, DEEP, SLAB)
            outs.append(pltpu.make_async_copy(speed, speed_out, out_sems.at[STEPS]))
            outs[0].start()
        leap(fields[moment + 1], fields[moment], fields[moment + 2], speed, along, margin, laps, moment)
        out = pltpu.make_async_copy(laps.at[moment, :, pl.ds(DEEP, SLAB)], lap_out.at[moment], out_sems.at[moment])
        out.start()
        outs.append(out)
        for shot in range(SHOTS_HERE):

            @pl.loop(0, src_counts[shot])
            def _(item, shot=shot):
                plane, depth, lane, which = unpack_entry(src[shot, item])
                amplitude = (2 * signs[shot, which] - 1).astype(jnp.float32) * wave[shot, moment]
                view = fields[moment + 2].at[shot, plane, pl.ds(depth, 1), :]
                view[...] = view[...] + jnp.where(ids == lane, amplitude, 0.0)

    for shot in range(SHOTS_HERE):

        def sample(group, state, shot=shot):
            state = list(state)
            for member in range(4):
                plane, depth, lane, which = unpack_entry(entries[shot, group * 4 + member])
                shift = (which - lane) & (NY - 1)
                hits = [ids == jnp.where(lane >= 0, which - half * NY, -1) for half in range(2)]
                for moment in range(STEPS):
                    line = fields[moment + 2][shot, plane, pl.ds(depth, 1), :]
                    line = pltpu.roll(line, shift, 1)
                    for half in range(2):
                        at = moment * 2 + half
                        state[at] = jnp.where(hits[half], line, state[at])
            return tuple(state)

        zero = jnp.zeros((1, NY), jnp.float32)
        state = lax.fori_loop(0, (counts[shot] + 3) >> 2, sample, (zero,) * (2 * STEPS))
        for moment in range(STEPS):
            for half in range(2):
                line = half * 8 + shot * STEPS + moment
                samples[line : line + 1, :] = state[moment * 2 + half]
    block = samples[...]
    for target in range(16):
        outgoing[target * 24 : target * 24 + 8, :] = noise[target * 8 : target * 8 + 8, :]
        outgoing[target * 24 + 8 : target * 24 + 24, :] = block
    for out in outs:
        out.wait()


def halo_rows(field):
    pairs = []
    for shot in range(SHOTS_HERE):
        for begin in (DEEP - 8, DEEP + SLAB):
            pairs.append(field.at[shot, pl.ds(begin, 8), pl.ds(PAD, NZ), :])
    return pairs


def adjoint_start_kernel(
    now, after, speed_in, low, high, lanes, earlier_out, halo_out, field, later, earlier, speed, along, sems
):
    copies = started(
        [
            *own_pairs(field, now),
            *halo_pairs(field, low, high, 0, DEEP),
            *own_pairs(later, after),
            *halo_pairs(later, low, high, SHOTS_HERE * DEEP, SHALLOW),
            (speed_in, speed),
        ],
        sems,
    )
    clear_pads([field])
    for copy in copies[:6]:
        copy.wait()
    margin = 4 * (STEPS - 1)
    along_lanes(field, lanes, along, margin)
    for copy in copies[6:]:
        copy.wait()
    outs = started([(rows, halo_out.at[place]) for place, rows in enumerate(halo_rows(field))], sems)
    for number, chunks in enumerate(((0, 3), (3, 5), (5, 7))):
        leap(field, later, earlier, speed, along, margin, chunks=chunks)
        rows = pl.ds(DEEP - margin + chunks[0] * CHUNK, (chunks[1] - chunks[0]) * CHUNK)
        source = earlier.at[:, rows, pl.ds(PAD, NZ), :]
        out = pltpu.make_async_copy(source, earlier_out.at[:, rows], sems.at[4 + number])
        out.start()
        outs.append(out)
    for copy in outs:
        copy.wait()


def adjoint_kernel(
    own, own_count, beyond, beyond_count,
    earlier, now, halo, speed_in, vel, laps_in, lanes, incoming, observed,
    tiles,
    *scratch,
):
    fields = [None, *scratch[: STEPS + 1]]
    laps, speed, along, plain, differences, misfit, sems = scratch[STEPS + 1 :]
    copies = started(
        [
            (
                earlier.at[:, pl.ds(DEEP - SHALLOW, SLAB + 2 * SHALLOW)],
                fields[2].at[:, pl.ds(DEEP - SHALLOW, SLAB + 2 * SHALLOW), pl.ds(PAD, NZ), :],
            ),
            *own_pairs(fields[1], now),
            *[(halo.at[place], rows) for place, rows in enumerate(halo_rows(fields[1]))],
            (speed_in, speed),
            (laps_in, laps),
            (vel, plain),
        ],
        sems,
    )
    total = incoming[8:24, :]
    for block in range(1, 16):
        total = total + incoming[block * 24 + 8 : block * 24 + 24, :]
    for shot in range(SHOTS_HERE):
        rows = slice(shot * STEPS, (shot + 1) * STEPS)
        for half in range(2):
            columns = slice(half * NY, (half + 1) * NY)
            differences[rows, columns] = (
                total[half * 8 + shot * STEPS : half * 8 + (shot + 1) * STEPS] - observed[shot, :, columns]
            )
    to_scalars = pltpu.make_async_copy(differences, misfit, sems.at[10])
    to_scalars.start()
    clear_pads(fields[2 : STEPS + 1])
    ids = lane_ids()
    for step in range(STEPS):
        moment = STEPS - step
        if step == 0:
            copies[0].wait()
            to_scalars.wait()
        else:
            margin = 4 * (STEPS - 1 - step)
            along_lanes(fields[step + 1], lanes, along, margin)
            if step == 1:
                for copy in copies[1:8]:
                    copy.wait()
            leap(fields[step + 1], fields[step], fields[step + 2], speed, along, margin)
        for entries, counts in ((own, own_count), (beyond, beyond_count))[: 2 if step < STEPS - 1 else 1]:
            for shot in range(SHOTS_HERE):

                @pl.loop(0, (counts[shot] + 3) >> 2)
                def _(group, entries=entries, shot=shot):
                    for member in range(4):
                        plane, depth, lane, which = unpack_entry(entries[shot, group * 4 + member])
                        value = misfit[shot * STEPS + moment - 1, which]
                        view = fields[step + 2].at[shot, plane, pl.ds(depth, 1), :]
                        view[...] = view[...] + jnp.where(ids == lane, value, 0.0)

    for copy in copies[8:]:
        copy.wait()
    for group in range(SLAB // 4):
        planes = []
        for plane in range(group * 4, group * 4 + 4):
            total = jnp.zeros((NZ, NY), jnp.float32)
            for shot in range(SHOTS_HERE):
                for step in range(STEPS):
                    total = total + (
                        fields[step + 2][shot, DEEP + plane, PAD : PAD + NZ, :]
                        * laps[STEPS - 1 - step, shot, plane]
                    )
            planes.append((2.0 * COURANT) * plain[plane] * total)
        tiles[pl.ds(group, NY, stride=SLAB // 4), :] = jnp.concatenate(planes, axis=0).T


def column_slices(source, target, turned):
    begin = pl.multiple_of(lax.axis_index("shot") * 16, 16)
    for group in range(SLAB // 4):
        turned[...] = source[group * NY : (group + 1) * NY, :].T
        target[pl.ds(group, 16, stride=SLAB // 4), :] = turned[pl.ds(begin, 16), :]


def apply_prior(columns, operators):
    lane = lax.broadcasted_iota(jnp.int32, (NY, NY), 1)
    blocks = []
    for place in range(4):
        turned = columns if place == 0 else pltpu.roll(columns, NY - 32 * place, 1)
        high = turned.astype(jnp.bfloat16).astype(jnp.float32)
        low = pltpu.roll(turned - high, 32, 1)
        blocks.append(jnp.where(lane < 32, high, low).astype(jnp.bfloat16))
    right = jnp.concatenate(blocks, axis=0)
    upper = dot(operators[0], right)
    lower = dot(operators[1], right)
    result = jnp.zeros((NY, NY), jnp.float32)
    for place in range(4):
        rows = slice(place * NY, (place + 1) * NY)
        value = (upper[rows] + lower[rows]) + pltpu.roll(upper[rows], NY - 32, 1)
        value = pltpu.roll(value, 32 * place, 1) if place else value
        result = jnp.where(lane // 32 == place, value, result)
    return result


def noise_kernel(step_size, incoming, operators, velocity, out, velocity_out, turned):
    column_slices(velocity, velocity_out, turned)
    columns = jnp.concatenate([incoming[block * 24 : block * 24 + 8, :] for block in range(16)], axis=0)
    scale = jnp.sqrt(jnp.full((8, NY), step_size[0], jnp.float32))[0:1]
    out[...] = scale * apply_prior(columns, operators)


def prior_kernel(step_size, received, noise, operators, out):
    total = received[0:NY, :]
    for part in range(1, 8):
        total = total + received[part * NY : (part + 1) * NY, :]
    out[...] = (-0.5 * step_size[0]) * apply_prior(total, operators) + noise[...]


def finish_kernel(returned, velocity, out):
    for group in range(SLAB // 4):
        rows = pl.ds(group, 16, stride=SLAB // 4)
        value = returned[rows, :] + velocity[rows, :]
        for place in range(4):
            turned = value if place == 0 else pltpu.roll(value, NY - 32 * place, 1)
            out[group * 4 + place] = turned[:, :NZ]


def shape(*dims, dtype=jnp.float32):
    return jax.ShapeDtypeStruct(dims, dtype)


def pin(values):
    return pltpu.with_memory_space_constraint(values, pltpu.VMEM)


def leave(*values):
    return [pltpu.with_memory_space_constraint(value, pltpu.HBM) for value in values]


def params():
    return pltpu.CompilerParams(vmem_limit_bytes=VMEM_LIMIT)


def neighbours(axis):
    count = lax.axis_size(axis)
    up = [(i, i + 1) for i in range(count - 1)]
    return up, [(b, a) for a, b in up]


def exchange(axis, to_high, to_low):
    up, down = neighbours(axis)
    return lax.ppermute(to_high, axis, up), lax.ppermute(to_low, axis, down)


def body(
    velocity,
    noise_field,
    step_size,
    field_prev,
    field_now,
    adjoint_next,
    adjoint_now,
    wavelet,
    source_cells,
    source_signs,
    record_cells,
    observed,
):
    lanes = jnp.asarray(lane_operator())
    squared, single = (jnp.asarray(operator) for operator in prior_operators())
    planes = SHOTS_HERE * (DEEP + SHALLOW)
    up, down = pl.pallas_call(
        edge_kernel,
        out_shape=(shape(planes + SHALLOW, NZ, NY),) * 2,
        in_specs=[ANY] * 3,
        out_specs=(ANY,) * 2,
        scratch_shapes=[
            *[pltpu.VMEM((planes + SHALLOW, NZ, NY), jnp.float32)] * 2,
            pltpu.SemaphoreType.DMA((2, 10)),
        ],
        name="edges",
    )(field_now, field_prev, velocity)
    low, high = exchange("dom", up, down)
    adjoint_edge, up, down = lax.optimization_barrier((adjoint_now, up, down))

    adj_up, adj_down, noise_tiles, *lists = pl.pallas_call(
        prepare_kernel,
        out_shape=(
            *(shape(planes, NZ, NY),) * 2,
            shape(NY, NY),
            *(shape(SHOTS_HERE, LIST, dtype=jnp.int32), shape(SHOTS_HERE, dtype=jnp.int32)) * 2,
            shape(SHOTS_HERE, 16, dtype=jnp.int32),
            shape(SHOTS_HERE, dtype=jnp.int32),
        ),
        in_specs=[SMEM] * 2 + [ANY] * 2 + [VMEM],
        out_specs=(ANY,) * 2 + (VMEM,) + (SMEM,) * 6,
        scratch_shapes=[
            pltpu.VMEM((NY, NY), jnp.float32),
            *[pltpu.VMEM((planes, NZ, NY), jnp.float32)] * 2,
            pltpu.SemaphoreType.DMA((2, 8)),
        ],
        name="prepare",
    )(
        record_cells, source_cells, adjoint_edge, adjoint_next,
        noise_field.reshape(SLAB * NZ, NY),
    )
    adj_low, adj_high = exchange("dom", adj_up, adj_down)

    fields = [pltpu.VMEM((SHOTS_HERE, ROWS, DEPTH, NY), jnp.float32)] * (STEPS + 2)
    speed = pltpu.VMEM((ROWS, NZ, NY), jnp.float32)
    along = pltpu.VMEM((SHOTS_HERE, ROWS, NZ, NY), jnp.float32)
    laplacians, outgoing, speed_sq = pl.pallas_call(
        forward_kernel,
        out_shape=(
            shape(STEPS, SHOTS_HERE, SLAB, NZ, NY), shape(16 * 24, NY), shape(ROWS, NZ, NY),
        ),
        in_specs=[SMEM] * 6 + [ANY] * 3 + [VMEM] * 4,
        out_specs=(ANY, VMEM, ANY),
        scratch_shapes=[
            *fields,
            pltpu.VMEM((STEPS, SHOTS_HERE, ROWS, NZ, NY), jnp.float32),
            speed,
            along,
            pltpu.VMEM((16, NY), jnp.float32),
            pltpu.SemaphoreType.DMA((5,)),
            pltpu.SemaphoreType.DMA((STEPS + 1,)),
        ],
        compiler_params=params(),
        name="forward_steps",
    )(
        *leave(*lists[:2], *lists[4:], source_signs, wavelet, field_now, field_prev, velocity),
        pin(low), pin(high), *leave(lanes, noise_tiles),
    )

    incoming = lax.all_to_all(outgoing.reshape(16, 24, NY), "dom", 0, 0, tiled=True).reshape(16 * 24, NY)

    field = fields[0]
    earlier, halo = pl.pallas_call(
        adjoint_start_kernel,
        out_shape=(shape(SHOTS_HERE, ROWS, NZ, NY), shape(SHOTS_HERE * 2, 8, NZ, NY)),
        in_specs=[ANY] * 5 + [VMEM],
        out_specs=(ANY,) * 2,
        scratch_shapes=[field, field, field, speed, along, pltpu.SemaphoreType.DMA((13,))],
        compiler_params=params(),
        name="adjoint_start",
    )(*leave(adjoint_now, adjoint_next, speed_sq), pin(adj_low), pin(adj_high), *leave(lanes))
    tiles = pl.pallas_call(
        adjoint_kernel,
        out_shape=shape(SLAB * NZ, NY),
        in_specs=[SMEM] * 4 + [ANY] * 6 + [VMEM] * 3,
        out_specs=VMEM,
        scratch_shapes=[
            *[field] * (STEPS + 1),
            pltpu.VMEM((STEPS, SHOTS_HERE, SLAB, NZ, NY), jnp.float32),
            speed,
            along,
            pltpu.VMEM((SLAB, NZ, NY), jnp.float32),
            pltpu.VMEM((SHOTS_HERE * STEPS, NREC), jnp.float32),
            pltpu.SMEM((SHOTS_HERE * STEPS, NREC), jnp.float32),
            pltpu.SemaphoreType.DMA((11,)),
        ],
        compiler_params=params(),
        name="adjoint_steps",
    )(
        *leave(*lists[:4], earlier, adjoint_now, halo, speed_sq, velocity, laplacians, lanes),
        pin(incoming), *leave(observed),
    )

    noise_update, velocity_tiles = pl.pallas_call(
        noise_kernel,
        out_shape=(shape(NY, NY),) * 2,
        in_specs=[SMEM] + [VMEM] * 3,
        out_specs=(VMEM,) * 2,
        scratch_shapes=[pltpu.VMEM((NY, NY), jnp.float32)],
        name="noise_prior",
    )(step_size, pin(incoming), single, velocity.reshape(SLAB * NZ, NY))

    received = lax.all_to_all(tiles.reshape(128, 8, NY), ("shot", "dom"), 0, 0, tiled=True)
    update = pl.pallas_call(
        prior_kernel,
        out_shape=shape(NY, NY),
        in_specs=[SMEM, VMEM, VMEM, VMEM],
        out_specs=VMEM,
        name="prior",
    )(step_size, pin(received.reshape(128 * 8, NY)), *leave(noise_update), pin(squared))
    returned = lax.all_to_all(update.reshape(16, 8, NY), "dom", 0, 0, tiled=True)
    out = pl.pallas_call(
        finish_kernel,
        out_shape=shape(SLAB, 16, NZ),
        in_specs=[VMEM, VMEM],
        out_specs=VMEM,
        name="finish",
    )(returned.reshape(NY, NY), velocity_tiles)
    return out.transpose(0, 2, 1)


def solution(mesh):
    placed = (
        P("dom", None, None),
        P("dom", None, None),
        P(),
        P("shot", "dom", None, None),
        P("shot", "dom", None, None),
        P("shot", "dom", None, None),
        P("shot", "dom", None, None),
        P("shot", None),
        P("shot", None),
        P("shot", None),
        P("shot", None),
        P("shot", None, None),
    )
    return jax.shard_map(
        body, mesh=mesh, in_specs=placed, out_specs=P("dom", None, "shot"), check_vma=False
    )
```
